32 devices in a mesh: dp: 8 (over y, x, core), seq: 4 (over z).
Axes of the slice: x: 2, y: 2, z: 4, core: 2. Of those that a mesh axis runs over, the one named last changes fastest.
Arguments:
- hidden: bfloat16 [8192, 1792], P(('dp', 'seq')), may hold values from -12.75 to 12.75
- depths: int32 [8192], P(('dp', 'seq')), may hold values from 1 to 3, as said below
- packed_slot_index: int32 [8192], P(('dp', 'seq')), may hold values from -1 to 511, as said below
- value_weight: bfloat16 [1792, 1024], P('dp'), may hold values from -0.125 to 0.125
- output_weight: bfloat16 [1024, 1792], P('dp'), may hold values from -0.1875 to 0.1875
- adapter_down_factor: bfloat16 [1792, 128], P('dp'), may hold values from -0.125 to 0.125
- adapter_up_factor: bfloat16 [1024, 128], P('dp'), may hold values from -0.5 to 0.5
- before_norm_gain: float32 [1792], replicated, may hold values from 0.1 to 1.9
- after_norm_gain: float32 [1792], replicated, may hold values from 0.1 to 1.9
- cotangent: bfloat16 [4096, 1792], P(('dp', 'seq')), may hold values from -6 to 6
Outputs:
- looped: bfloat16 [4096, 1792], P(('dp', 'seq'))
- grad_hidden: bfloat16 [8192, 1792], P(('dp', 'seq'))
- down_factor_gradient: float32 [1792, 128], P('dp', 'seq')
- up_factor_gradient: float32 [1024, 128], P('dp', 'seq')
The draws below stay inside these ranges and needn't reach their ends.
Inputs may be any that keep to these rules, and one draw needn't show every extreme that they name: `depths`: of the 1024 tokens of one dp index exactly 512 have depth 2 or 3, and all 256 tokens of one seq index are among them. -1 exactly where depths is 1. Over the tokens of one dp index with depth 2 or 3 the slots are a permutation of 0 to 511; packed_slot_index // 128 is the seq index that holds the token's packed row. At most 64 tokens of one device have slots of one seq index, and exactly 64 do in every dp index.
All inputs are finite; a program needn't handle non-finite values.
Results may differ from the reference program's by a relative error of at most 0.01.
Values may be sent and summed in bfloat16 or wider, within the bound.
A program may use at most 64 MiB of HBM per device.

```python
import math
import jax
import jax.numpy as jnp
from jax import lax

MODEL_WIDTH = 1792
VALUE_WIDTH = 1024
LOW_RANK_SIZE = 128
TOK_DEV = 256
GROUP_TOKENS = 1024
TOKENS = 8192
ACT_DEV = 128
GROUP_ROWS = 512
ALL_ACTIVE = 4096


def routing(key):
    base_key = jax.random.fold_in(key, 7)
    key_busy, key_pick, key_place, key_deep, key_turn = jax.random.split(base_key, 5)
    seq_count = GROUP_TOKENS // TOK_DEV
    groups = TOKENS // GROUP_TOKENS
    busy_dev = jax.random.randint(key_busy, (groups,), 0, seq_count)
    other_rows = (seq_count - 1) * TOK_DEV
    needed = GROUP_ROWS - TOK_DEV
    shuffled = jax.vmap(lambda one_key: jax.random.permutation(one_key, other_rows))(jax.random.split(key_pick, groups))
    chosen = (shuffled < needed).reshape(groups, seq_count - 1, TOK_DEV)
    device_ids = jnp.arange(seq_count, dtype=jnp.int32)[None, :]
    is_busy = device_ids == busy_dev[:, None]
    other_rank = jnp.clip(device_ids - (device_ids > busy_dev[:, None]).astype(jnp.int32), 0, seq_count - 2)
    picked = jnp.take_along_axis(chosen, jnp.broadcast_to(other_rank[:, :, None], (groups, seq_count, TOK_DEV)), axis=1)
    active = jnp.where(is_busy[:, :, None], True, picked).reshape(groups, GROUP_TOKENS)
    active_int = active.astype(jnp.int32)
    order_in = jnp.cumsum(active_int, axis=1) - active_int
    turn = jax.random.randint(key_turn, (groups, 1), 0, seq_count)
    dest_dev = (order_in + turn) % seq_count
    window = jnp.minimum(order_in // seq_count, ACT_DEV - 1)
    placing = jax.vmap(lambda one_key: jax.random.permutation(one_key, ACT_DEV))(jax.random.split(key_place, groups * seq_count))
    flat_place = placing.reshape(groups, seq_count * ACT_DEV).astype(jnp.int32)
    dest_pos = jnp.take_along_axis(flat_place, dest_dev * ACT_DEV + window, axis=1)
    slots = jnp.where(active, dest_dev * ACT_DEV + dest_pos, -1)
    deeper = jax.random.randint(key_deep, (groups, GROUP_TOKENS), 2, 4)
    depth_draw = jnp.where(active, deeper, 1)
    return (depth_draw.reshape(TOKENS).astype(jnp.int32), slots.reshape(TOKENS).astype(jnp.int32))


def draw_depths(key, part):
    return routing(key)[0]


def draw_packed_slot_index(key, part):
    return routing(key)[1]


def draw_hidden(key, part):
    key_base, key_rows, key_cols = jax.random.split(jax.random.fold_in(key, 11), 3)
    row_scale = jnp.exp(jax.random.uniform(key_rows, (TOKENS, 1), jnp.float32, math.log(0.6), math.log(1.7)))
    col_scale = jnp.exp(jax.random.uniform(key_cols, (1, MODEL_WIDTH), jnp.float32, math.log(0.4), math.log(2.5)))
    base_draw = jax.random.truncated_normal(key_base, -3.0, 3.0, (TOKENS, MODEL_WIDTH), jnp.float32)
    return (base_draw * row_scale * col_scale).astype(jnp.bfloat16)


def steps_of(own_key, extent, cuts, low, largest):
    level, own = 1.0, jax.random.fold_in(own_key, 6)
    for axis_at, blocks in cuts:
        draws = jnp.exp(jax.random.uniform(jax.random.fold_in(own, axis_at), (blocks,), jnp.float32, low / len(cuts), largest / len(cuts)))
        level = level * jnp.repeat(draws, extent[axis_at] // blocks).reshape([-1 if axis == axis_at else 1 for axis in range(len(extent))])
    return level


def centred(own_key, extent, spread, most, shards=(), kind=jnp.bfloat16):
    gain = steps_of(own_key, extent, shards, -0.22, 0.18) if shards else 1.0
    result = jax.random.normal(own_key, extent, jnp.float32) * spread * gain
    return jnp.minimum(jnp.maximum(result, -most), most).astype(kind)


def setup_inputs(seed: int = 0) -> dict:
    splits = jax.random.split(jax.random.key(seed), 11)
    return {
        "hidden": draw_hidden(jax.random.fold_in(splits[10], 71), 0),
        "depths": draw_depths(jax.random.fold_in(splits[10], 71), 0),
        "packed_slot_index": draw_packed_slot_index(jax.random.fold_in(splits[10], 71), 0),
        "value_weight": centred(splits[3], (MODEL_WIDTH, VALUE_WIDTH), MODEL_WIDTH ** -0.5, 0.125, ((0, 8),)),
        "output_weight": centred(splits[4], (VALUE_WIDTH, MODEL_WIDTH), VALUE_WIDTH ** -0.5, 0.1875, ((0, 8),)),
        "adapter_down_factor": centred(splits[5], (MODEL_WIDTH, LOW_RANK_SIZE), MODEL_WIDTH ** -0.5, 0.125, ((0, 8),)),
        "adapter_up_factor": centred(splits[6], (VALUE_WIDTH, LOW_RANK_SIZE), LOW_RANK_SIZE ** -0.5, 0.5, ((0, 8),)),
        "before_norm_gain": jnp.clip(1.0 + 0.18 * jax.random.normal(splits[7], (MODEL_WIDTH,), jnp.float32), 0.1, 1.9),
        "after_norm_gain": jnp.clip(1.0 + 0.18 * jax.random.normal(splits[8], (MODEL_WIDTH,), jnp.float32), 0.1, 1.9),
        "cotangent": centred(splits[9], (ALL_ACTIVE, MODEL_WIDTH), 1.0, 6.0, ((0, 32),)),
    }


epsilon = 1e-06

def contract_final_axis(left, right):
    return lax.dot_general(left, right, (((1,), (1,)), ((), ())), preferred_element_type=jnp.float32)

def contract_first(left, right):
    return lax.dot_general(left, right, (((0,), (0,)), ((), ())), preferred_element_type=jnp.float32)

def layer_forward(input_rows, cotangent_rows, value_weight, output_weight, adapter_down_factor, adapter_up_factor, before_norm_gain, after_norm_gain):
    x_float = input_rows.astype(jnp.float32)
    inv_pre = lax.rsqrt(lax.optimization_barrier(jnp.mean(x_float * x_float, axis=-1, keepdims=True)) + epsilon)
    whitened = x_float * inv_pre
    normalized_rows = (whitened * before_norm_gain).astype(jnp.bfloat16)
    rank_reduced = jnp.dot(normalized_rows, adapter_down_factor, preferred_element_type=jnp.float32).astype(jnp.bfloat16)
    projected_rows = (jnp.dot(normalized_rows, value_weight, preferred_element_type=jnp.float32) + contract_final_axis(rank_reduced, adapter_up_factor)).astype(jnp.bfloat16)
    mixed_out = jnp.dot(projected_rows, output_weight, preferred_element_type=jnp.float32)
    inv_post = lax.rsqrt(lax.optimization_barrier(jnp.mean(mixed_out * mixed_out, axis=-1, keepdims=True)) + epsilon)
    shaped = mixed_out * inv_post
    looped = (x_float + shaped * after_norm_gain).astype(jnp.bfloat16)
    cot_float = cotangent_rows.astype(jnp.float32)
    grad_shaped = cot_float * after_norm_gain
    grad_mixed = (inv_post * (grad_shaped - shaped * lax.optimization_barrier(jnp.mean(grad_shaped * shaped, axis=-1, keepdims=True)))).astype(jnp.bfloat16)
    value_gradient = contract_final_axis(grad_mixed, output_weight).astype(jnp.bfloat16)
    low_rank_gradient = jnp.dot(value_gradient, adapter_up_factor, preferred_element_type=jnp.float32).astype(jnp.bfloat16)
    normalized_gradient = contract_final_axis(value_gradient, value_weight) + contract_final_axis(low_rank_gradient, adapter_down_factor)
    grad_white = normalized_gradient * before_norm_gain
    gradient_rows = (cot_float + inv_pre * (grad_white - whitened * lax.optimization_barrier(jnp.mean(grad_white * whitened, axis=-1, keepdims=True)))).astype(jnp.bfloat16)
    down_factor_gradient = contract_first(normalized_rows, low_rank_gradient)
    up_factor_gradient = contract_first(value_gradient, rank_reduced)
    return (looped, gradient_rows, down_factor_gradient, up_factor_gradient)

def reference(hidden, depths, packed_slot_index, value_weight, output_weight, adapter_down_factor, adapter_up_factor, before_norm_gain, after_norm_gain, cotangent):
    active = depths >= 2
    group_of = jnp.arange(TOKENS, dtype=jnp.int32) // GROUP_TOKENS
    target = jnp.where(active, group_of * GROUP_ROWS + packed_slot_index, ALL_ACTIVE).astype(jnp.int32)
    packed = jnp.zeros((ALL_ACTIVE, MODEL_WIDTH), jnp.bfloat16).at[target].set(hidden, mode='drop')
    groups = ALL_ACTIVE // GROUP_ROWS

    def step_fn(totals, pieces):
        entering_rows, incoming_cotangent = pieces
        looped, gradient_rows, down_factor_gradient, up_factor_gradient = layer_forward(entering_rows, incoming_cotangent, value_weight, output_weight, adapter_down_factor, adapter_up_factor, before_norm_gain, after_norm_gain)
        return ((totals[0] + down_factor_gradient, totals[1] + up_factor_gradient), (looped, gradient_rows))
    init = (jnp.zeros((MODEL_WIDTH, LOW_RANK_SIZE), jnp.float32), jnp.zeros((VALUE_WIDTH, LOW_RANK_SIZE), jnp.float32))
    totals, outputs = lax.scan(step_fn, init, (packed.reshape(groups, GROUP_ROWS, MODEL_WIDTH), cotangent.reshape(groups, GROUP_ROWS, MODEL_WIDTH)))
    looped = outputs[0].reshape(ALL_ACTIVE, MODEL_WIDTH)
    gradient_rows = outputs[1].reshape(ALL_ACTIVE, MODEL_WIDTH)
    picked = jnp.take(gradient_rows, jnp.minimum(target, ALL_ACTIVE - 1), axis=0)
    grad_hidden = jnp.where(active[:, None], picked, jnp.zeros((), jnp.bfloat16))
    grad_scale = 1.0 / math.sqrt(ALL_ACTIVE)
    return (looped, grad_hidden, totals[0] * grad_scale, totals[1] * grad_scale)
```

```python
import functools
import math

import jax
import jax.numpy as jnp
from jax import lax
from jax.experimental import pallas as pl
from jax.experimental.pallas import tpu as pltpu
from jax.sharding import PartitionSpec as P

epsilon = 1e-06


def contract_final_axis(left, right):
    return lax.dot_general(
        left, right, (((1,), (1,)), ((), ())), preferred_element_type=jnp.float32
    )


def contract_first(left, right):
    return lax.dot_general(
        left, right, (((0,), (0,)), ((), ())), preferred_element_type=jnp.float32
    )


def layer_forward(
    input_rows,
    cotangent_rows,
    value_weight,
    output_weight,
    adapter_down_factor,
    adapter_up_factor,
    before_norm_gain,
    after_norm_gain,
):
    x_float = input_rows.astype(jnp.float32)
    inv_pre = lax.rsqrt(jnp.mean(x_float * x_float, axis=-1, keepdims=True) + epsilon)
    whitened = x_float * inv_pre
    normalized_rows = (whitened * before_norm_gain).astype(jnp.bfloat16)
    rank_reduced = jnp.dot(
        normalized_rows, adapter_down_factor, preferred_element_type=jnp.float32
    ).astype(jnp.bfloat16)
    projected_rows = (
        jnp.dot(normalized_rows, value_weight, preferred_element_type=jnp.float32)
        + contract_final_axis(rank_reduced, adapter_up_factor)
    ).astype(jnp.bfloat16)
    mixed_out = jnp.dot(projected_rows, output_weight, preferred_element_type=jnp.float32)
    inv_post = lax.rsqrt(jnp.mean(mixed_out * mixed_out, axis=-1, keepdims=True) + epsilon)
    shaped = mixed_out * inv_post
    looped = (x_float + shaped * after_norm_gain).astype(jnp.bfloat16)
    cot_float = cotangent_rows.astype(jnp.float32)
    grad_shaped = cot_float * after_norm_gain
    grad_mixed = (
        inv_post * (grad_shaped - shaped * jnp.mean(grad_shaped * shaped, axis=-1, keepdims=True))
    ).astype(jnp.bfloat16)
    value_gradient = contract_final_axis(grad_mixed, output_weight).astype(jnp.bfloat16)
    low_rank_gradient = jnp.dot(
        value_gradient, adapter_up_factor, preferred_element_type=jnp.float32
    ).astype(jnp.bfloat16)
    normalized_gradient = contract_final_axis(value_gradient, value_weight) + contract_final_axis(
        low_rank_gradient, adapter_down_factor
    )
    grad_white = normalized_gradient * before_norm_gain
    gradient_rows = (
        cot_float
        + inv_pre
        * (grad_white - whitened * jnp.mean(grad_white * whitened, axis=-1, keepdims=True))
    ).astype(jnp.bfloat16)
    down_factor_gradient = contract_first(normalized_rows, low_rank_gradient)
    up_factor_gradient = contract_first(value_gradient, rank_reduced)
    return (looped, gradient_rows, down_factor_gradient, up_factor_gradient)


def general_body(
    hidden,
    depths,
    packed_slot_index,
    value_weight,
    output_weight,
    adapter_down_factor,
    adapter_up_factor,
    before_norm_gain,
    after_norm_gain,
    cotangent,
):
    seq_count = lax.axis_size("seq")
    own_index = lax.axis_index("seq")
    tok_count = hidden.shape[0]
    act_rows = cotangent.shape[0]
    value_full, out_full, down_full, up_full = (
        lax.all_gather(value_weight, "dp", axis=0, tiled=True),
        lax.all_gather(output_weight, "dp", axis=0, tiled=True),
        lax.all_gather(adapter_down_factor, "dp", axis=0, tiled=True),
        lax.all_gather(adapter_up_factor, "dp", axis=0, tiled=True),
    )
    depth_all, slot_all = (
        lax.all_gather(depths, "seq", axis=0, tiled=True),
        lax.all_gather(packed_slot_index, "seq", axis=0, tiled=True),
    )
    active_all = depth_all >= 2
    dest_all = jnp.where(active_all, slot_all // act_rows, -1)
    pos_all = jnp.where(active_all, slot_all % act_rows, 0)
    mine = active_all & (dest_all == own_index)
    active = depths >= 2
    zero_row = jnp.zeros((), jnp.bfloat16)
    rows_all = lax.all_gather(hidden, "seq", axis=0, tiled=True)
    source = (
        jnp.zeros((act_rows,), jnp.int32)
        .at[jnp.where(mine, pos_all, act_rows)]
        .set(jnp.arange(seq_count * tok_count, dtype=jnp.int32), mode="drop")
    )
    packed = jnp.take(rows_all, source, axis=0)
    looped, gradient_rows, down_factor_gradient, up_factor_gradient = layer_forward(
        packed,
        cotangent,
        value_full,
        out_full,
        down_full,
        up_full,
        before_norm_gain,
        after_norm_gain,
    )
    grads_all = lax.all_gather(gradient_rows, "seq", axis=0, tiled=True)
    picked = jnp.take(grads_all, jnp.maximum(packed_slot_index, 0), axis=0)
    grad_hidden = jnp.where(active[:, None], picked, zero_row)
    grad_scale = 1.0 / math.sqrt(seq_count * act_rows * lax.axis_size("dp"))
    down_term = down_factor_gradient * grad_scale
    up_term = up_factor_gradient * grad_scale
    down_mid, up_mid = (
        lax.psum_scatter(
            down_term.astype(jnp.bfloat16), "seq", scatter_dimension=1, tiled=True
        ).astype(jnp.float32),
        lax.psum_scatter(
            up_term.astype(jnp.bfloat16), "seq", scatter_dimension=1, tiled=True
        ).astype(jnp.float32),
    )
    down_sum, up_sum = (
        lax.psum_scatter(down_mid, "dp", scatter_dimension=0, tiled=True),
        lax.psum_scatter(up_mid, "dp", scatter_dimension=0, tiled=True),
    )
    return (looped, grad_hidden, down_sum, up_sum)


MESH = pl.DeviceIdType.MESH
BF, F32 = jnp.bfloat16, jnp.float32
CAP = 64
TILE = 256


def dot(left, right, left_axis=1, right_axis=0):
    return lax.dot_general(
        left, right, (((left_axis,), (right_axis,)), ((), ())), preferred_element_type=F32
    )


def fused_kernel(
    slot_hbm, depth_hbm, gain_b_hbm, gain_a_hbm, hidden_hbm, cot_hbm, wv_in, wo_in, dn_in, up_in,
    grad_out, loop_out, down_out, up_out,
    slot_v, depth_v, gain_b_v, gain_a_v, hid, cot, wvd, wou, psend, precv, csend, crecv,
    gain_b, gain_a, xs, normed, acc, low, mixed, gm, gvl, looped, lprecv, place_t, place, unplace,
    unplace_t, lsend, lpair, lsum, lrecv, zsend, zrecv, stat_a, stat_b, stat_c,
    w_send, w_recv, p_send, p_recv, c_send, c_recv, o_send, o_recv, l_send, l_recv,
    z_send, z_recv, loc,
):
    dp, seq = lax.axis_index("dp"), lax.axis_index("seq")
    n_dp, n_seq = 8, 4
    width = hid.shape[1]
    value_width = acc.shape[1]
    core, x, y = dp % 2, (dp // 2) % 2, dp // 4
    nbr_x, nbr_y, sib = dp + 2 - 4 * x, dp + 4 - 8 * y, dp + 1 - 2 * core
    diag = nbr_x + 4 - 8 * y
    to_sib = 1 - 2 * core
    odd = seq % 2
    seq_mate = seq + 1 - 2 * odd
    v_rows, o_rows = wv_in.shape[0], wo_in.shape[0]
    tiles = width // TILE

    def lanes(n, size=TILE):
        return pl.ds(pl.multiple_of(n * size, size), size)

    own_v = pl.ds(pl.multiple_of(dp * v_rows, 16), v_rows)
    own_o = pl.ds(pl.multiple_of(dp * o_rows, 16), o_rows)
    moves = [
        (slot_hbm, slot_v),
        (depth_hbm, depth_v),
        (wv_in, wvd.at[own_v, pl.ds(0, value_width)]),
        (dn_in, wvd.at[own_v, pl.ds(value_width, 128)]),
        (wo_in, wou.at[own_o, pl.ds(0, width)]),
        (up_in, wou.at[own_o, pl.ds(width, 128)]),
        (hidden_hbm, hid),
        (cot_hbm, cot),
        (gain_b_hbm, gain_b_v),
        (gain_a_hbm, gain_a_v),
    ]
    local = [pltpu.make_async_copy(a, b, loc.at[i]) for i, (a, b) in enumerate(moves)]
    for copy in local:
        copy.start()

    barrier = pltpu.get_barrier_semaphore()
    for k in range(1, n_dp):
        pl.semaphore_signal(barrier, inc=1, device_id=((dp + k) % n_dp, seq), device_id_type=MESH)
    for k in range(1, n_seq):
        pl.semaphore_signal(barrier, inc=1, device_id=(dp, (seq + k) % n_seq), device_id_type=MESH)

    local[0].wait()
    local[1].wait()
    tok = hid.shape[0]
    rows = n_seq * CAP
    slots = jnp.concatenate([slot_v[i : i + 1, :] for i in range(tok // 128)], axis=1)
    depth = jnp.concatenate([depth_v[i : i + 1, :] for i in range(tok // 128)], axis=1)
    act = depth >= 2
    dest = jnp.where(act, slots // 128, -1)
    where_to = lax.broadcasted_iota(jnp.int32, (8, tok), 0) == dest
    earlier = (
        lax.broadcasted_iota(jnp.int32, (tok, tok), 0)
        < lax.broadcasted_iota(jnp.int32, (tok, tok), 1)
    ).astype(F32).astype(BF)
    counts = dot(where_to.astype(F32).astype(BF), earlier)
    rank = jnp.sum(jnp.where(where_to, counts, 0.0), axis=0, keepdims=True)
    row_of = jnp.where(act, dest.astype(F32) * CAP + rank, -1.0)
    picked = (lax.broadcasted_iota(jnp.int32, (rows, tok), 0).astype(F32) == row_of).astype(F32)
    position = jnp.where(act, slots - dest * 128 + 1, 0).astype(F32)
    pos_col = jnp.sum(picked * position, axis=1, keepdims=True) - 1.0
    psend[...] = jnp.broadcast_to(pos_col, (rows, 128)).astype(BF)
    for copy in local[2:6]:
        copy.wait()

    pl.semaphore_wait(barrier, n_dp - 1 + n_seq - 1)

    pending = []

    def block(owner, size=CAP):
        return pl.ds(pl.multiple_of(owner * size, 16), size)

    def exchange(src_buf, dst_buf, sends, recvs):
        for k in (2, 1, 3):
            target = (seq + k) % n_seq
            copy = pltpu.make_async_remote_copy(
                src_ref=src_buf.at[block(target), :], dst_ref=dst_buf.at[block(seq), :],
                send_sem=sends.at[k], recv_sem=recvs.at[k], device_id=(dp, target),
                device_id_type=MESH,
            )
            copy.start()
            pending.append(copy)
        dst_buf[block(seq), :] = src_buf[block(seq), :]

    def arrive(dst_buf, sends, recvs):
        for k in (1, 2, 3):
            origin = (seq + n_seq - k) % n_seq
            here = dst_buf.at[block(origin), :]
            pltpu.make_async_remote_copy(
                src_ref=here, dst_ref=here, send_sem=sends.at[k], recv_sem=recvs.at[k],
                device_id=(dp, origin), device_id_type=MESH,
            ).wait_recv()

    exchange(psend, precv, p_send, p_recv)

    arrays = ((wvd, v_rows), (wou, o_rows))

    def region(a, owner, kind):
        full, size = arrays[a]
        half = size // 2
        first = -(-half // 32) * 16
        start, count = {
            "all": (0, size),
            "a": (odd * half, first),
            "b": (odd * half + first, half - first),
            "o": ((1 - odd) * half, half),
            "a2": ((1 - odd) * half, first),
            "b2": ((1 - odd) * half + first, half - first),
        }[kind]
        return full.at[pl.ds(pl.multiple_of(owner * size + start, 16), count), :]

    def piece(a, number, owner, kind, target):
        here = region(a, owner, kind)
        return pltpu.make_async_remote_copy(
            src_ref=here, dst_ref=here, send_sem=w_send.at[a * 21 + number],
            recv_sem=w_recv.at[a * 21 + number], device_id=target, device_id_type=MESH,
        )

    on_x, on_y, on_sib, on_z = (nbr_x, seq), (nbr_y, seq), (sib, seq), (dp, seq_mate)

    def send(*args):
        copy = piece(*args)
        copy.start()
        pending.append(copy)

    def got(a, number, owner, kind):
        piece(a, number, owner, kind, on_sib).wait_recv()

    def own_first(a):
        send(a, 0, dp, "a", on_x)
        send(a, 3, dp, "b", on_y)

    def own_second(a):
        send(a, 1, dp, "b", on_x)
        send(a, 4, dp, "a", on_y)

    def own_third(a):
        send(a, 2, dp, "o", on_x)
        send(a, 5, dp, "o", on_y)

    def forward_first(a):
        got(a, 0, nbr_x, "a")
        send(a, 7, nbr_x, "a", on_y)
        send(a, 9, nbr_x, "a", on_sib)
        got(a, 3, nbr_y, "b")
        send(a, 8, nbr_y, "b", on_x)
        send(a, 12, nbr_y, "b", on_sib)

    def forward_second(a):
        got(a, 1, nbr_x, "b")
        send(a, 10, nbr_x, "b", on_sib)
        got(a, 4, nbr_y, "a")
        send(a, 13, nbr_y, "a", on_sib)

    def forward_diag(a):
        got(a, 7, diag, "a")
        send(a, 15, diag, "a", on_z)
        send(a, 17, diag, "a", on_sib)
        got(a, 8, diag, "b")
        send(a, 16, diag, "b", on_z)
        send(a, 18, diag, "b", on_sib)

    def forward_third(a):
        got(a, 2, nbr_x, "o")
        send(a, 11, nbr_x, "o", on_sib)
        got(a, 5, nbr_y, "o")
        send(a, 14, nbr_y, "o", on_sib)

    def forward_last(a):
        got(a, 15, diag, "a2")
        send(a, 19, diag, "a2", on_sib)
        got(a, 16, diag, "b2")
        send(a, 20, diag, "b2", on_sib)

    def finish_x(a):
        got(a, 9, nbr_x + to_sib, "a")
        got(a, 10, nbr_x + to_sib, "b")
        got(a, 11, nbr_x + to_sib, "o")

    def finish_y(a):
        got(a, 12, nbr_y + to_sib, "b")
        got(a, 13, nbr_y + to_sib, "a")
        got(a, 14, nbr_y + to_sib, "o")

    def finish_diag(a):
        got(a, 17, diag + to_sib, "a")
        got(a, 18, diag + to_sib, "b")
        got(a, 19, diag + to_sib, "a2")
        got(a, 20, diag + to_sib, "b2")

    own_first(0)
    own_first(1)
    own_second(0)
    send(0, 6, dp, "all", on_sib)
    send(1, 6, dp, "all", on_sib)

    place[...] = picked.astype(BF)
    place_t[...] = picked.T.astype(BF)
    for copy in local[6:]:
        copy.wait()
    for i in range(width // 128):
        gain_b[:, i * 128 : (i + 1) * 128] = gain_b_v[i : i + 1, :]
        gain_a[:, i * 128 : (i + 1) * 128] = gain_a_v[i : i + 1, :]

    def fold(v):
        return v[:, :128] + v[:, 128:]

    def spread(v):
        return jnp.broadcast_to(v, (rows, 128))

    def wide(v):
        return jnp.concatenate([v, v], axis=1)

    arrive(precv, p_send, p_recv)
    at_lane = lax.broadcasted_iota(jnp.int32, (rows, 128), 1).astype(F32)
    chosen = (precv[...].astype(F32) == at_lane).astype(F32)
    unplace[...] = chosen.astype(BF)

    @pl.loop(0, tiles)
    def _(n):
        csend[:, lanes(n)] = dot(unplace[...], cot[:, lanes(n)]).astype(BF)

    exchange(csend, crecv, c_send, c_recv)
    unplace_t[...] = chosen.T.astype(BF)

    stat_a[...] = jnp.zeros_like(stat_a)

    @pl.loop(0, tiles)
    def _(n):
        v = dot(place[...], hid[:, lanes(n)])
        xs[:, lanes(n)] = v.astype(BF)
        stat_a[...] += fold(v * v)

    inv_pre = lax.rsqrt(jnp.sum(stat_a[...], axis=1, keepdims=True) / width + epsilon)
    stat_a[...] = spread(inv_pre)

    @pl.loop(0, tiles)
    def _(n):
        v = xs[:, lanes(n)].astype(F32) * wide(stat_a[...])
        normed[:, lanes(n)] = (v * gain_b[:, lanes(n)]).astype(BF)

    forward_first(0)
    own_third(0)
    forward_first(1)
    own_second(1)
    own_third(1)
    forward_second(0)
    forward_diag(0)
    forward_third(0)
    forward_diag(1)
    forward_last(0)
    got(0, 6, sib, "all")
    finish_x(0)
    finish_y(0)
    finish_diag(0)

    low[...] = dot(normed[...], wvd[:, value_width:]).astype(BF)

    @pl.loop(0, value_width // TILE)
    def _(n):
        acc[:, lanes(n)] = dot(normed[...], wvd[:, lanes(n)])

    def mix(member, init=False, last=False):
        chip = member // 2
        at = pl.ds(pl.multiple_of(chip * 2 * o_rows, 256), 2 * o_rows)
        part = (acc[:, at] + dot(low[...], wou[at, width:], 1, 1)).astype(BF)

        @pl.loop(0, tiles)
        def _(n):
            m = dot(part, wou[at, lanes(n)])
            if not init:
                m += mixed[:, lanes(n)]
            mixed[:, lanes(n)] = m
            if last:
                stat_b[...] += fold(m * m)

    stat_b[...] = jnp.zeros_like(stat_b)
    got(1, 6, sib, "all")
    mix(dp, init=True)
    forward_second(1)
    forward_last(1)
    forward_third(1)
    finish_diag(1)
    mix(diag)
    finish_x(1)
    mix(nbr_x)
    finish_y(1)
    mix(nbr_y, last=True)

    inv_post = lax.rsqrt(jnp.sum(stat_b[...], axis=1, keepdims=True) / width + epsilon)
    stat_b[...] = spread(inv_post)

    @pl.loop(0, tiles)
    def _(n):
        shaped = mixed[:, lanes(n)] * wide(stat_b[...])
        v = xs[:, lanes(n)].astype(F32) + shaped * gain_a[:, lanes(n)]
        looped[:, lanes(n)] = v.astype(BF)

    exchange(looped, lprecv, o_send, o_recv)
    arrive(crecv, c_send, c_recv)
    stat_c[...] = jnp.zeros_like(stat_c)

    @pl.loop(0, tiles)
    def _(n):
        g = crecv[:, lanes(n)].astype(F32) * gain_a[:, lanes(n)]
        stat_c[...] += fold(g * (mixed[:, lanes(n)] * wide(stat_b[...])))

    pull = jnp.sum(stat_c[...], axis=1, keepdims=True) / width
    stat_c[...] = spread(pull)

    @pl.loop(0, tiles)
    def _(n):
        g = crecv[:, lanes(n)].astype(F32) * gain_a[:, lanes(n)]
        inv = wide(stat_b[...])
        shaped = mixed[:, lanes(n)] * inv
        gm[:, lanes(n)] = (inv * (g - shaped * wide(stat_c[...]))).astype(BF)

    @pl.loop(0, value_width // TILE)
    def _(n):
        gvl[:, lanes(n)] = dot(gm[...], wou[lanes(n), :width], 1, 1).astype(BF)

    grad_low = dot(gvl[:, :value_width], wou[:, width:]).astype(BF)
    gvl[:, value_width:] = grad_low

    down_term = dot(grad_low, normed[...], 0, 0).astype(BF)
    up_term = dot(low[...], gvl[:, :value_width], 0, 0).astype(BF)
    spare = jnp.zeros((128, lsend.shape[3] - v_rows - o_rows), BF)
    for owner in range(n_dp):
        lsend[owner // 2, owner % 2] = jnp.concatenate(
            [
                down_term[:, owner * v_rows : (owner + 1) * v_rows],
                spare,
                up_term[:, owner * o_rows : (owner + 1) * o_rows],
            ],
            axis=1,
        )
    pair = pltpu.make_async_remote_copy(
        src_ref=lsend.at[:, 1 - core], dst_ref=lpair, send_sem=l_send.at[0],
        recv_sem=l_recv.at[0], device_id=on_sib, device_id_type=MESH,
    )
    pair.start()
    pending.append(pair)

    stat_c[...] = jnp.zeros_like(stat_c)

    @pl.loop(0, tiles)
    def _(n):
        g = dot(gvl[...], wvd[lanes(n), :], 1, 1) * gain_b[:, lanes(n)]
        mixed[:, lanes(n)] = g
        stat_c[...] += fold(g * (xs[:, lanes(n)].astype(F32) * wide(stat_a[...])))

    pair.wait_recv()
    lsum[...] = (lsend[:, core].astype(F32) + lpair[...].astype(F32)).astype(BF)
    chip = dp // 2
    for k, target in ((1, nbr_x), (2, nbr_y), (3, diag)):
        copy = pltpu.make_async_remote_copy(
            src_ref=lsum.at[target // 2], dst_ref=lrecv.at[k], send_sem=l_send.at[k],
            recv_sem=l_recv.at[k], device_id=(target, seq), device_id_type=MESH,
        )
        copy.start()
        pending.append(copy)

    pull = jnp.sum(stat_c[...], axis=1, keepdims=True) / width
    stat_c[...] = spread(pull)

    @pl.loop(0, tiles)
    def _(n):
        inv = wide(stat_a[...])
        whitened = xs[:, lanes(n)].astype(F32) * inv
        g = crecv[:, lanes(n)].astype(F32) + inv * (
            mixed[:, lanes(n)] - whitened * wide(stat_c[...])
        )
        grad_out[:, lanes(n)] = dot(place_t[...], g.astype(BF)).astype(BF)

    for k, origin in ((1, nbr_x), (2, nbr_y), (3, diag)):
        here = lrecv.at[k]
        pltpu.make_async_remote_copy(
            src_ref=here, dst_ref=here, send_sem=l_send.at[k], recv_sem=l_recv.at[k],
            device_id=(origin, seq), device_id_type=MESH,
        ).wait_recv()
    total = lsum[chip].astype(F32)
    for k in (1, 2, 3):
        total += lrecv[k].astype(F32)
    zsend[...] = total.astype(BF)
    cols = down_out.shape[0]
    for k in range(1, n_seq):
        target = (seq + k) % n_seq
        copy = pltpu.make_async_remote_copy(
            src_ref=zsend.at[block(target, cols), :], dst_ref=zrecv.at[seq],
            send_sem=z_send.at[k], recv_sem=z_recv.at[k], device_id=(dp, target),
            device_id_type=MESH,
        )
        copy.start()
        pending.append(copy)
    zrecv[seq] = zsend[block(seq, cols), :]
    for k in range(1, n_seq):
        origin = (seq + n_seq - k) % n_seq
        here = zrecv.at[origin]
        pltpu.make_async_remote_copy(
            src_ref=here, dst_ref=here, send_sem=z_send.at[k], recv_sem=z_recv.at[k],
            device_id=(dp, origin), device_id_type=MESH,
        ).wait_recv()
    grad_scale = 1.0 / math.sqrt(n_seq * cot.shape[0] * n_dp)
    part = [zrecv[i].astype(F32) for i in range(n_seq)]
    mine = ((part[0] + part[1]) + (part[2] + part[3])) * grad_scale
    down_out[...] = mine[:, :v_rows]
    up_out[...] = mine[:, lsend.shape[3] - o_rows :]

    arrive(lprecv, o_send, o_recv)

    @pl.loop(0, tiles)
    def _(n):
        loop_out[:, lanes(n)] = dot(unplace_t[...], lprecv[:, lanes(n)]).astype(BF)

    for copy in pending:
        copy.wait_send()


def store_kernel(*refs):
    sources, targets, sems = refs[:4], refs[4:8], refs[8]
    copies = [pltpu.make_async_copy(sources[i], targets[i], sems.at[i]) for i in range(4)]
    for copy in copies:
        copy.start()
    for copy in copies:
        copy.wait()


def fused_body(
    hidden, depths, packed_slot_index, value_weight, output_weight, adapter_down_factor,
    adapter_up_factor, before_norm_gain, after_norm_gain, cotangent,
):
    tok, width = hidden.shape
    act = cotangent.shape[0]
    n_dp, n_seq = lax.axis_size("dp"), lax.axis_size("seq")
    v_rows, value_width = value_weight.shape
    o_rows = output_weight.shape[0]
    rank = adapter_up_factor.shape[1]
    cols = rank // n_seq
    lead = -(-v_rows // 128) * 128 + o_rows
    vm, hbm = pl.BlockSpec(memory_space=pltpu.VMEM), pl.BlockSpec(memory_space=pltpu.HBM)
    dma = pltpu.SemaphoreType.DMA
    rows = n_seq * CAP

    def b16(*shape):
        return pltpu.VMEM(shape, BF)

    def f32(*shape):
        return pltpu.VMEM(shape, F32)

    shapes = (
        jax.ShapeDtypeStruct((tok, width), BF),
        jax.ShapeDtypeStruct((act, width), BF),
        jax.ShapeDtypeStruct((cols, v_rows), F32),
        jax.ShapeDtypeStruct((cols, o_rows), F32),
    )
    results = pl.pallas_call(
        fused_kernel,
        out_shape=shapes,
        in_specs=[hbm] * 10,
        out_specs=(vm,) * 4,
        scratch_shapes=[
            pltpu.VMEM((tok // 128, 128), jnp.int32),
            pltpu.VMEM((tok // 128, 128), jnp.int32),
            f32(width // 128, 128),
            f32(width // 128, 128),
            b16(tok, width),
            b16(act, width),
            b16(v_rows * n_dp, value_width + rank),
            b16(o_rows * n_dp, width + rank),
            b16(rows, 128),
            b16(rows, 128),
            b16(rows, width),
            b16(rows, width),
            f32(1, width),
            f32(1, width),
            b16(rows, width),
            b16(rows, width),
            f32(rows, value_width),
            b16(rows, rank),
            f32(rows, width),
            b16(rows, width),
            b16(rows, value_width + rank),
            b16(rows, width),
            b16(rows, width),
            b16(tok, rows),
            b16(rows, tok),
            b16(rows, 128),
            b16(128, rows),
            b16(n_dp // 2, 2, rank, lead),
            b16(n_dp // 2, rank, lead),
            b16(n_dp // 2, rank, lead),
            b16(4, rank, lead),
            b16(rank, lead),
            b16(n_seq, cols, lead),
            f32(rows, 128),
            f32(rows, 128),
            f32(rows, 128),
            dma((42,)), dma((42,)), dma((4,)), dma((4,)), dma((4,)), dma((4,)), dma((4,)), dma((4,)),
            dma((8,)), dma((8,)), dma((4,)), dma((4,)), dma((10,)),
        ],
        compiler_params=pltpu.CompilerParams(
            collective_id=0, has_side_effects=True, vmem_limit_bytes=56 << 20
        ),
        name="layer",
    )(
        packed_slot_index.reshape(tok // 128, 128),
        depths.reshape(tok // 128, 128),
        before_norm_gain.reshape(width // 128, 128),
        after_norm_gain.reshape(width // 128, 128),
        hidden,
        cotangent,
        value_weight,
        output_weight,
        adapter_down_factor,
        adapter_up_factor,
    )
    grad, looped, down, up = results
    return looped, grad, down.T, up.T


def body(*arrays):
    fits = (
        lax.axis_size("dp") == 8
        and lax.axis_size("seq") == 4
        and arrays[0].shape[0] == 4 * CAP
        and arrays[9].shape[0] == 128
        and arrays[0].shape[1] % 256 == 0
        and arrays[3].shape[1] % 256 == 0
        and all(arrays[i].shape[0] % 32 == 0 for i in (3, 4, 5, 6))
        and arrays[4].shape[0] == 128
        and arrays[6].shape[1] == 128
    )
    return (fused_body if fits else general_body)(*arrays)


def solution(mesh):
    placed = (
        P(("dp", "seq"), None),
        P(("dp", "seq")),
        P(("dp", "seq")),
        P("dp", None),
        P("dp", None),
        P("dp", None),
        P("dp", None),
        P(),
        P(),
        P(("dp", "seq"), None),
    )
    return jax.shard_map(
        body,
        mesh=mesh,
        in_specs=placed,
        out_specs=(P(("dp", "seq"), None), P(("dp", "seq"), None), P("dp", "seq"), P("dp", "seq")),
        check_vma=False,
    )
```

```python
import functools
import math

import jax
import jax.numpy as jnp
from jax import lax
from jax.experimental import pallas as pl
from jax.experimental.pallas import tpu as pltpu
from jax.sharding import PartitionSpec as P

epsilon = 1e-06


def contract_final_axis(left, right):
    return lax.dot_general(
        left, right, (((1,), (1,)), ((), ())), preferred_element_type=jnp.float32
    )


def contract_first(left, right):
    return lax.dot_general(
        left, right, (((0,), (0,)), ((), ())), preferred_element_type=jnp.float32
    )


def layer_forward(
    input_rows,
    cotangent_rows,
    value_weight,
    output_weight,
    adapter_down_factor,
    adapter_up_factor,
    before_norm_gain,
    after_norm_gain,
):
    x_float = input_rows.astype(jnp.float32)
    inv_pre = lax.rsqrt(jnp.mean(x_float * x_float, axis=-1, keepdims=True) + epsilon)
    whitened = x_float * inv_pre
    normalized_rows = (whitened * before_norm_gain).astype(jnp.bfloat16)
    rank_reduced = jnp.dot(
        normalized_rows, adapter_down_factor, preferred_element_type=jnp.float32
    ).astype(jnp.bfloat16)
    projected_rows = (
        jnp.dot(normalized_rows, value_weight, preferred_element_type=jnp.float32)
        + contract_final_axis(rank_reduced, adapter_up_factor)
    ).astype(jnp.bfloat16)
    mixed_out = jnp.dot(projected_rows, output_weight, preferred_element_type=jnp.float32)
    inv_post = lax.rsqrt(jnp.mean(mixed_out * mixed_out, axis=-1, keepdims=True) + epsilon)
    shaped = mixed_out * inv_post
    looped = (x_float + shaped * after_norm_gain).astype(jnp.bfloat16)
    cot_float = cotangent_rows.astype(jnp.float32)
    grad_shaped = cot_float * after_norm_gain
    grad_mixed = (
        inv_post * (grad_shaped - shaped * jnp.mean(grad_shaped * shaped, axis=-1, keepdims=True))
    ).astype(jnp.bfloat16)
    value_gradient = contract_final_axis(grad_mixed, output_weight).astype(jnp.bfloat16)
    low_rank_gradient = jnp.dot(
        value_gradient, adapter_up_factor, preferred_element_type=jnp.float32
    ).astype(jnp.bfloat16)
    normalized_gradient = contract_final_axis(value_gradient, value_weight) + contract_final_axis(
        low_rank_gradient, adapter_down_factor
    )
    grad_white = normalized_gradient * before_norm_gain
    gradient_rows = (
        cot_float
        + inv_pre
        * (grad_white - whitened * jnp.mean(grad_white * whitened, axis=-1, keepdims=True))
    ).astype(jnp.bfloat16)
    down_factor_gradient = contract_first(normalized_rows, low_rank_gradient)
    up_factor_gradient = contract_first(value_gradient, rank_reduced)
    return (looped, gradient_rows, down_factor_gradient, up_factor_gradient)


def general_body(
    hidden,
    depths,
    packed_slot_index,
    value_weight,
    output_weight,
    adapter_down_factor,
    adapter_up_factor,
    before_norm_gain,
    after_norm_gain,
    cotangent,
):
    seq_count = lax.axis_size("seq")
    own_index = lax.axis_index("seq")
    tok_count = hidden.shape[0]
    act_rows = cotangent.shape[0]
    value_full, out_full, down_full, up_full = (
        lax.all_gather(value_weight, "dp", axis=0, tiled=True),
        lax.all_gather(output_weight, "dp", axis=0, tiled=True),
        lax.all_gather(adapter_down_factor, "dp", axis=0, tiled=True),
        lax.all_gather(adapter_up_factor, "dp", axis=0, tiled=True),
    )
    depth_all, slot_all = (
        lax.all_gather(depths, "seq", axis=0, tiled=True),
        lax.all_gather(packed_slot_index, "seq", axis=0, tiled=True),
    )
    active_all = depth_all >= 2
    dest_all = jnp.where(active_all, slot_all // act_rows, -1)
    pos_all = jnp.where(active_all, slot_all % act_rows, 0)
    mine = active_all & (dest_all == own_index)
    active = depths >= 2
    zero_row = jnp.zeros((), jnp.bfloat16)
    rows_all = lax.all_gather(hidden, "seq", axis=0, tiled=True)
    source = (
        jnp.zeros((act_rows,), jnp.int32)
        .at[jnp.where(mine, pos_all, act_rows)]
        .set(jnp.arange(seq_count * tok_count, dtype=jnp.int32), mode="drop")
    )
    packed = jnp.take(rows_all, source, axis=0)
    looped, gradient_rows, down_factor_gradient, up_factor_gradient = layer_forward(
        packed,
        cotangent,
        value_full,
        out_full,
        down_full,
        up_full,
        before_norm_gain,
        after_norm_gain,
    )
    grads_all = lax.all_gather(gradient_rows, "seq", axis=0, tiled=True)
    picked = jnp.take(grads_all, jnp.maximum(packed_slot_index, 0), axis=0)
    grad_hidden = jnp.where(active[:, None], picked, zero_row)
    grad_scale = 1.0 / math.sqrt(seq_count * act_rows * lax.axis_size("dp"))
    down_term = down_factor_gradient * grad_scale
    up_term = up_factor_gradient * grad_scale
    down_mid, up_mid = (
        lax.psum_scatter(
            down_term.astype(jnp.bfloat16), "seq", scatter_dimension=1, tiled=True
        ).astype(jnp.float32),
        lax.psum_scatter(
            up_term.astype(jnp.bfloat16), "seq", scatter_dimension=1, tiled=True
        ).astype(jnp.float32),
    )
    down_sum, up_sum = (
        lax.psum_scatter(down_mid, "dp", scatter_dimension=0, tiled=True),
        lax.psum_scatter(up_mid, "dp", scatter_dimension=0, tiled=True),
    )
    return (looped, grad_hidden, down_sum, up_sum)


MESH = pl.DeviceIdType.MESH
BF, F32 = jnp.bfloat16, jnp.float32
CAP = 64
TILE = 256
EARLY = 16
LATE = CAP - EARLY


def dot(left, right, left_axis=1, right_axis=0):
    return lax.dot_general(
        left, right, (((left_axis,), (right_axis,)), ((), ())), preferred_element_type=F32
    )


def fused_kernel(
    slot_hbm, depth_hbm, gain_b_hbm, gain_a_hbm, hidden_hbm, cot_hbm, wv_in, wo_in, dn_in, up_in,
    grad_hbm, loop_hbm, place_hbm, unplace_hbm, down_hbm, up_hbm,
    slot_v, depth_v, gain_b_v, gain_a_v, hid, cot, wvd, wo, up, psend, precv, csend, crecv,
    gain_b, gain_a, xs, normed, proj, low, mixed, gm, gvl, looped, place_t, place, unplace,
    unplace_t, lsend, lpair, lsum, lrecv, zsend, zrecv, stat_a, stat_b, stat_c, stat_e,
    hid_e, proj_e, mixed_e, looped_e, grad_v, down_v, up_v,
    w_send, w_recv, u_send, u_recv, p_send, p_recv, c_send, c_recv, o_send, o_recv,
    h_send, h_recv, q_send, q_recv, l_send, l_recv, z_send, z_recv, loc, fin,
):
    dp, seq = lax.axis_index("dp"), lax.axis_index("seq")
    n_dp, n_seq = 8, 4
    width = hid.shape[1]
    value_width = proj.shape[1]
    core, x, y = dp % 2, (dp // 2) % 2, dp // 4
    nbr_x, nbr_y, sib = dp + 2 - 4 * x, dp + 4 - 8 * y, dp + 1 - 2 * core
    diag = nbr_x + 4 - 8 * y
    to_sib = 1 - 2 * core
    odd = seq % 2
    seq_mate = seq + 1 - 2 * odd
    v_rows, o_rows = wv_in.shape[0], wo_in.shape[0]
    tiles = width // TILE

    def lanes(n, size=TILE):
        return pl.ds(pl.multiple_of(n * size, size), size)

    own_v = pl.ds(pl.multiple_of(dp * v_rows, 16), v_rows)
    own_o = pl.ds(pl.multiple_of(dp * o_rows, 16), o_rows)
    moves = [
        (slot_hbm, slot_v),
        (depth_hbm, depth_v),
        (wv_in, wvd.at[own_v, pl.ds(0, value_width)]),
        (dn_in, wvd.at[own_v, pl.ds(value_width, 128)]),
        (wo_in, wo.at[own_o, :]),
        (up_in, up.at[own_o, :]),
        (hidden_hbm, hid),
        (cot_hbm, cot),
        (gain_b_hbm, gain_b_v),
        (gain_a_hbm, gain_a_v),
    ]
    local = [pltpu.make_async_copy(a, b, loc.at[i]) for i, (a, b) in enumerate(moves)]
    for copy in local:
        copy.start()

    barrier = pltpu.get_barrier_semaphore()
    for k in range(1, n_dp):
        pl.semaphore_signal(barrier, inc=1, device_id=((dp + k) % n_dp, seq), device_id_type=MESH)
    for k in range(1, n_seq):
        pl.semaphore_signal(barrier, inc=1, device_id=(dp, (seq + k) % n_seq), device_id_type=MESH)

    local[0].wait()
    local[1].wait()
    tok = hid.shape[0]
    rows = n_seq * CAP
    slots = jnp.concatenate([slot_v[i : i + 1, :] for i in range(tok // 128)], axis=1)
    depth = jnp.concatenate([depth_v[i : i + 1, :] for i in range(tok // 128)], axis=1)
    act = depth >= 2
    dest = jnp.where(act, slots // 128, -1)
    where_to = lax.broadcasted_iota(jnp.int32, (8, tok), 0) == dest
    earlier = (
        lax.broadcasted_iota(jnp.int32, (tok, tok), 0)
        < lax.broadcasted_iota(jnp.int32, (tok, tok), 1)
    ).astype(F32).astype(BF)
    counts = dot(where_to.astype(F32).astype(BF), earlier)
    rank = jnp.sum(jnp.where(where_to, counts, 0.0), axis=0, keepdims=True)
    row_of = jnp.where(act, dest.astype(F32) * CAP + rank, -1.0)
    picked = (lax.broadcasted_iota(jnp.int32, (rows, tok), 0).astype(F32) == row_of).astype(F32)
    position = jnp.where(act, slots - dest * 128 + 1, 0).astype(F32)
    pos_col = jnp.sum(picked * position, axis=1, keepdims=True) - 1.0
    psend[...] = jnp.broadcast_to(pos_col, (rows, 128)).astype(BF)
    for copy in local[2:6]:
        copy.wait()

    pl.semaphore_wait(barrier, n_dp - 1 + n_seq - 1)

    pending = []

    def block(owner, size=CAP):
        return pl.ds(pl.multiple_of(owner * size, 16), size)

    peers = (seq_mate, (seq + 2) % n_seq, n_seq - 1 - seq)

    def row_copy(src_buf, dst_buf, sends, recvs, k, first=0, count=CAP, stride=CAP):
        return pltpu.make_async_remote_copy(
            src_ref=src_buf.at[pl.ds(pl.multiple_of(peers[k] * CAP + first, 16), count), :],
            dst_ref=dst_buf.at[pl.ds(pl.multiple_of(seq * stride, 16), count), :],
            send_sem=sends.at[k], recv_sem=recvs.at[k], device_id=(dp, peers[k]),
            device_id_type=MESH,
        )

    def exchange(*args, **kw):
        for k in (1, 2, 0):
            copy = row_copy(*args, k, **kw)
            copy.start()
            pending.append(copy)

    def arrive(dst_buf, sends, recvs, count=CAP, stride=CAP):
        for k in (0, 1, 2):
            here = dst_buf.at[pl.ds(pl.multiple_of(peers[k] * stride, 16), count), :]
            pltpu.make_async_remote_copy(
                src_ref=here, dst_ref=here, send_sem=sends.at[k], recv_sem=recvs.at[k],
                device_id=(dp, peers[k]), device_id_type=MESH,
            ).wait_recv()

    exchange(psend, precv, p_send, p_recv)
    precv[block(seq), :] = psend[block(seq), :]

    arrays = ((wvd, v_rows), (wo, o_rows))

    def region(a, owner, kind):
        full, size = arrays[a]
        half = size // 2
        first = -(-half // 32) * 16
        start, count = {
            "all": (0, size),
            "a": (odd * half, first),
            "b": (odd * half + first, half - first),
            "o": ((1 - odd) * half, half),
            "a2": ((1 - odd) * half, first),
            "b2": ((1 - odd) * half + first, half - first),
        }[kind]
        return full.at[pl.ds(pl.multiple_of(owner * size + start, 16), count), :]

    def piece(a, number, owner, kind, target):
        here = region(a, owner, kind)
        return pltpu.make_async_remote_copy(
            src_ref=here, dst_ref=here, send_sem=w_send.at[a * 21 + number],
            recv_sem=w_recv.at[a * 21 + number], device_id=target, device_id_type=MESH,
        )

    on_x, on_y, on_sib, on_z = (nbr_x, seq), (nbr_y, seq), (sib, seq), (dp, seq_mate)

    def send(*args):
        copy = piece(*args)
        copy.start()
        pending.append(copy)

    def got(a, number, owner, kind):
        piece(a, number, owner, kind, on_sib).wait_recv()

    def own_first(a):
        send(a, 0, dp, "a", on_x)
        send(a, 3, dp, "b", on_y)

    def own_second(a):
        send(a, 1, dp, "b", on_x)
        send(a, 4, dp, "a", on_y)

    def own_third(a):
        send(a, 2, dp, "o", on_x)
        send(a, 5, dp, "o", on_y)

    def forward_first(a):
        got(a, 0, nbr_x, "a")
        send(a, 7, nbr_x, "a", on_y)
        send(a, 9, nbr_x, "a", on_sib)
        got(a, 3, nbr_y, "b")
        send(a, 8, nbr_y, "b", on_x)
        send(a, 12, nbr_y, "b", on_sib)

    def forward_second(a):
        got(a, 1, nbr_x, "b")
        send(a, 10, nbr_x, "b", on_sib)
        got(a, 4, nbr_y, "a")
        send(a, 13, nbr_y, "a", on_sib)

    def forward_diag(a):
        got(a, 7, diag, "a")
        send(a, 15, diag, "a", on_z)
        send(a, 17, diag, "a", on_sib)
        got(a, 8, diag, "b")
        send(a, 16, diag, "b", on_z)
        send(a, 18, diag, "b", on_sib)

    def forward_third(a):
        got(a, 2, nbr_x, "o")
        send(a, 11, nbr_x, "o", on_sib)
        got(a, 5, nbr_y, "o")
        send(a, 14, nbr_y, "o", on_sib)

    def forward_last(a):
        got(a, 15, diag, "a2")
        send(a, 19, diag, "a2", on_sib)
        got(a, 16, diag, "b2")
        send(a, 20, diag, "b2", on_sib)

    def finish_x(a):
        got(a, 9, nbr_x + to_sib, "a")
        got(a, 10, nbr_x + to_sib, "b")
        got(a, 11, nbr_x + to_sib, "o")

    def finish_y(a):
        got(a, 12, nbr_y + to_sib, "b")
        got(a, 13, nbr_y + to_sib, "a")
        got(a, 14, nbr_y + to_sib, "o")

    def finish_diag(a):
        got(a, 17, diag + to_sib, "a")
        got(a, 18, diag + to_sib, "b")
        got(a, 19, diag + to_sib, "a2")
        got(a, 20, diag + to_sib, "b2")

    def up_copy(number, owner, target):
        here = up.at[pl.ds(pl.multiple_of(owner * o_rows, 16), o_rows), :]
        return pltpu.make_async_remote_copy(
            src_ref=here, dst_ref=here, send_sem=u_send.at[number], recv_sem=u_recv.at[number],
            device_id=target, device_id_type=MESH,
        )

    def up_send(number, owner, target):
        copy = up_copy(number, owner, target)
        copy.start()
        pending.append(copy)

    own_first(0)
    up_send(0, dp, on_x)
    up_send(1, dp, on_y)
    up_send(2, dp, (diag, seq))
    up_send(3, dp, on_sib)
    own_first(1)
    own_second(0)
    send(0, 6, dp, "all", on_sib)
    send(1, 6, dp, "all", on_sib)

    place[...] = picked.astype(BF)
    place_t[...] = picked.T.astype(BF)
    for copy in local[6:]:
        copy.wait()
    for i in range(width // 128):
        gain_b[:, i * 128 : (i + 1) * 128] = gain_b_v[i : i + 1, :]
        gain_a[:, i * 128 : (i + 1) * 128] = gain_a_v[i : i + 1, :]

    def fold(v):
        return v[:, :128] + v[:, 128:]

    def spread(v):
        return jnp.broadcast_to(v, (rows, 128))

    def wide(v):
        return jnp.concatenate([v, v], axis=1)

    arrive(precv, p_send, p_recv)
    at_lane = lax.broadcasted_iota(jnp.int32, (rows, 128), 1).astype(F32)
    chosen = (precv[...].astype(F32) == at_lane).astype(F32)
    unplace[...] = chosen.astype(BF)

    @pl.loop(0, tiles, unroll=True)
    def _(n):
        csend[:, lanes(n)] = dot(unplace[...], cot[:, lanes(n)]).astype(BF)

    cot_copies = [row_copy(csend, crecv, c_send, c_recv, k) for k in range(3)]
    pending.extend(cot_copies)
    inner = (seq == 1) | (seq == 2)

    @pl.when(jnp.logical_not(inner))
    def _():
        cot_copies[1].start()
        cot_copies[2].start()

    crecv[block(seq), :] = csend[block(seq), :]
    unplace_t[...] = chosen.T.astype(BF)
    saved = [
        pltpu.make_async_copy(place_t, place_hbm, fin.at[0]),
        pltpu.make_async_copy(unplace_t, unplace_hbm, fin.at[1]),
    ]
    for copy in saved:
        copy.start()

    stat_a[...] = jnp.zeros_like(stat_a)

    @pl.loop(0, tiles, unroll=True)
    def _(n):
        v = dot(place[...], hid[:, lanes(n)])
        xs[:, lanes(n)] = v.astype(BF)
        stat_a[...] += fold(v * v)

    inv_pre = lax.rsqrt(jnp.sum(stat_a[...], axis=1, keepdims=True) / width + epsilon)
    stat_a[...] = spread(inv_pre)

    @pl.loop(0, tiles, unroll=True)
    def _(n):
        v = xs[:, lanes(n)].astype(F32) * wide(stat_a[...])
        normed[:, lanes(n)] = (v * gain_b[:, lanes(n)]).astype(BF)

    forward_first(0)
    own_third(0)
    forward_first(1)
    own_second(1)
    own_third(1)
    for k, owner in enumerate((nbr_x, nbr_y, diag)):
        up_copy(k, owner, on_sib).wait_recv()
        up_send(4 + k, owner, on_sib)
    forward_second(0)

    forward_diag(0)

    @pl.when(inner)
    def _():
        cot_copies[1].start()
        cot_copies[2].start()

    forward_third(0)
    forward_diag(1)
    cot_copies[0].start()
    exchange(xs, hid_e, h_send, h_recv, first=LATE, count=EARLY, stride=EARLY)
    own_early = pl.ds(pl.multiple_of(seq * CAP + LATE, 16), EARLY)
    hid_e[block(seq, EARLY), :] = xs[own_early, :]
    forward_last(0)
    got(0, 6, sib, "all")
    finish_x(0)
    finish_y(0)
    finish_diag(0)

    low[...] = dot(normed[...], wvd[:, value_width:]).astype(BF)
    up_copy(3, sib, on_sib).wait_recv()
    for k, owner in enumerate((nbr_x, nbr_y, diag)):
        up_copy(4 + k, owner + to_sib, on_sib).wait_recv()

    @pl.loop(0, value_width // TILE, unroll=True)
    def _(n):
        proj[:, lanes(n)] = (
            dot(normed[...], wvd[:, lanes(n)]) + dot(low[...], up[lanes(n), :], 1, 1)
        ).astype(BF)

    exchange(proj, proj_e, q_send, q_recv, first=LATE, count=EARLY, stride=EARLY)
    proj_e[block(seq, EARLY), :] = proj[own_early, :]

    def mix(member, init=False, last=False):
        at = pl.ds(pl.multiple_of(member // 2 * 2 * o_rows, 256), 2 * o_rows)

        @pl.loop(0, tiles, unroll=True)
        def _(n):
            m = dot(proj[:, at], wo[at, lanes(n)])
            if not init:
                m += mixed[:, lanes(n)]
            mixed[:, lanes(n)] = m
            if last:
                stat_b[...] += fold(m * m)

    stat_b[...] = jnp.zeros_like(stat_b)
    got(1, 6, sib, "all")
    mix(dp, init=True)
    forward_second(1)
    forward_last(1)
    forward_third(1)
    finish_diag(1)
    mix(diag)
    finish_x(1)
    mix(nbr_x)
    finish_y(1)
    mix(nbr_y, last=True)

    inv_post = lax.rsqrt(jnp.sum(stat_b[...], axis=1, keepdims=True) / width + epsilon)
    stat_b[...] = spread(inv_post)

    @pl.loop(0, tiles, unroll=True)
    def _(n):
        shaped = mixed[:, lanes(n)] * wide(stat_b[...])
        v = xs[:, lanes(n)].astype(F32) + shaped * gain_a[:, lanes(n)]
        looped[:, lanes(n)] = v.astype(BF)

    exchange(looped, loop_hbm, o_send, o_recv, count=LATE)
    saved.append(
        pltpu.make_async_copy(
            looped.at[block(seq), :].at[pl.ds(0, LATE), :],
            loop_hbm.at[pl.ds(pl.multiple_of(seq * CAP, 16), LATE), :],
            fin.at[2],
        )
    )
    saved[-1].start()
    arrive(crecv, c_send, c_recv)
    stat_c[...] = jnp.zeros_like(stat_c)

    @pl.loop(0, tiles, unroll=True)
    def _(n):
        g = crecv[:, lanes(n)].astype(F32) * gain_a[:, lanes(n)]
        stat_c[...] += fold(g * (mixed[:, lanes(n)] * wide(stat_b[...])))

    pull = jnp.sum(stat_c[...], axis=1, keepdims=True) / width
    stat_c[...] = spread(pull)

    @pl.loop(0, tiles, unroll=True)
    def _(n):
        g = crecv[:, lanes(n)].astype(F32) * gain_a[:, lanes(n)]
        inv = wide(stat_b[...])
        shaped = mixed[:, lanes(n)] * inv
        gm[:, lanes(n)] = (inv * (g - shaped * wide(stat_c[...]))).astype(BF)

    @pl.loop(0, value_width // TILE, unroll=True)
    def _(n):
        gvl[:, lanes(n)] = dot(gm[...], wo[lanes(n), :], 1, 1).astype(BF)

    grad_low = dot(gvl[:, :value_width], up[...]).astype(BF)
    gvl[:, value_width:] = grad_low

    down_term = dot(grad_low, normed[...], 0, 0).astype(BF)
    up_term = dot(low[...], gvl[:, :value_width], 0, 0).astype(BF)
    spare = jnp.zeros((128, lsend.shape[3] - v_rows - o_rows), BF)
    for owner in range(n_dp):
        lsend[owner // 2, owner % 2] = jnp.concatenate(
            [
                down_term[:, owner * v_rows : (owner + 1) * v_rows],
                spare,
                up_term[:, owner * o_rows : (owner + 1) * o_rows],
            ],
            axis=1,
        )
    pair = pltpu.make_async_remote_copy(
        src_ref=lsend.at[:, 1 - core], dst_ref=lpair, send_sem=l_send.at[0],
        recv_sem=l_recv.at[0], device_id=on_sib, device_id_type=MESH,
    )
    pair.start()
    pending.append(pair)

    stat_c[...] = jnp.zeros_like(stat_c)

    @pl.loop(0, tiles, unroll=True)
    def _(n):
        g = dot(gvl[...], wvd[lanes(n), :], 1, 1) * gain_b[:, lanes(n)]
        mixed[:, lanes(n)] = g
        stat_c[...] += fold(g * (xs[:, lanes(n)].astype(F32) * wide(stat_a[...])))

    pair.wait_recv()
    lsum[...] = (lsend[:, core].astype(F32) + lpair[...].astype(F32)).astype(BF)
    chip = dp // 2
    for k, target in ((1, nbr_x), (2, nbr_y), (3, diag)):
        copy = pltpu.make_async_remote_copy(
            src_ref=lsum.at[target // 2], dst_ref=lrecv.at[k], send_sem=l_send.at[k],
            recv_sem=l_recv.at[k], device_id=(target, seq), device_id_type=MESH,
        )
        copy.start()
        pending.append(copy)

    pull = jnp.sum(stat_c[...], axis=1, keepdims=True) / width
    stat_c[...] = spread(pull)

    @pl.loop(0, tiles, unroll=True)
    def _(n):
        inv = wide(stat_a[...])
        whitened = xs[:, lanes(n)].astype(F32) * inv
        g = crecv[:, lanes(n)].astype(F32) + inv * (
            mixed[:, lanes(n)] - whitened * wide(stat_c[...])
        )
        grad_v[:, lanes(n)] = g.astype(BF)

    saved.append(pltpu.make_async_copy(grad_v, grad_hbm, fin.at[3]))
    saved[-1].start()

    arrive(hid_e, h_send, h_recv, count=EARLY, stride=EARLY)
    arrive(proj_e, q_send, q_recv, count=EARLY, stride=EARLY)
    stat_e[...] = jnp.zeros_like(stat_e)

    @pl.loop(0, tiles, unroll=True)
    def _(n):
        m = dot(proj_e[...], wo[:, lanes(n)])
        mixed_e[:, lanes(n)] = m
        stat_e[...] += fold(m * m)

    inv_early = lax.rsqrt(jnp.sum(stat_e[...], axis=1, keepdims=True) / width + epsilon)
    stat_e[...] = jnp.broadcast_to(inv_early, stat_e.shape)

    @pl.loop(0, tiles, unroll=True)
    def _(n):
        shaped = mixed_e[:, lanes(n)] * wide(stat_e[...])
        v = hid_e[:, lanes(n)].astype(F32) + shaped * gain_a[:, lanes(n)]
        looped_e[:, lanes(n)] = v.astype(BF)

    for i in range(n_seq):
        saved.append(
            pltpu.make_async_copy(
                looped_e.at[pl.ds(i * EARLY, EARLY), :],
                loop_hbm.at[pl.ds(i * CAP + LATE, EARLY), :],
                fin.at[4 + i],
            )
        )
        saved[-1].start()

    for k, origin in ((1, nbr_x), (2, nbr_y), (3, diag)):
        here = lrecv.at[k]
        pltpu.make_async_remote_copy(
            src_ref=here, dst_ref=here, send_sem=l_send.at[k], recv_sem=l_recv.at[k],
            device_id=(origin, seq), device_id_type=MESH,
        ).wait_recv()
    total = lsum[chip].astype(F32)
    for k in (1, 2, 3):
        total += lrecv[k].astype(F32)
    zsend[...] = total.astype(BF)
    cols = down_v.shape[0]
    for k in range(1, n_seq):
        target = (seq + k) % n_seq
        copy = pltpu.make_async_remote_copy(
            src_ref=zsend.at[block(target, cols), :], dst_ref=zrecv.at[seq],
            send_sem=z_send.at[k], recv_sem=z_recv.at[k], device_id=(dp, target),
            device_id_type=MESH,
        )
        copy.start()
        pending.append(copy)
    zrecv[seq] = zsend[block(seq, cols), :]
    for k in range(1, n_seq):
        origin = (seq + n_seq - k) % n_seq
        here = zrecv.at[origin]
        pltpu.make_async_remote_copy(
            src_ref=here, dst_ref=here, send_sem=z_send.at[k], recv_sem=z_recv.at[k],
            device_id=(dp, origin), device_id_type=MESH,
        ).wait_recv()
    grad_scale = 1.0 / math.sqrt(n_seq * cot.shape[0] * n_dp)
    part = [zrecv[i].astype(F32) for i in range(n_seq)]
    mine = ((part[0] + part[1]) + (part[2] + part[3])) * grad_scale
    down_v[...] = mine[:, :v_rows]
    up_v[...] = mine[:, lsend.shape[3] - o_rows :]
    saved.append(pltpu.make_async_copy(down_v, down_hbm, fin.at[8]))
    saved.append(pltpu.make_async_copy(up_v, up_hbm, fin.at[9]))
    saved[-2].start()
    saved[-1].start()

    arrive(loop_hbm, o_send, o_recv, count=LATE)
    for copy in pending:
        copy.wait_send()
    for copy in saved:
        copy.wait()


def store_kernel(
    grad_in, loop_in, place_in, unplace_in, down_in, up_in, looped_hbm, grad_hbm, down_hbm, up_hbm,
    grad_v, loop_v, place_v, unplace_v, down_v, up_v, looped_o, grad_o, ins, outs,
):
    width = grad_in.shape[1]
    tiles = width // TILE
    small = [
        (place_in, place_v), (unplace_in, unplace_v), (down_in, down_v), (up_in, up_v),
    ]
    loads = [pltpu.make_async_copy(a, b, ins.at[i]) for i, (a, b) in enumerate(small)]
    for n in range(tiles):
        at = pl.ds(n * TILE, TILE)
        for k, (a, b) in enumerate(((grad_in, grad_v), (loop_in, loop_v))):
            loads.append(
                pltpu.make_async_copy(a.at[:, at], b.at[:, at], ins.at[4 + 2 * n + k])
            )
    for copy in loads:
        copy.start()
    stores = []

    def store(src, dst):
        stores.append(pltpu.make_async_copy(src, dst, outs.at[len(stores)]))
        stores[-1].start()

    for copy in loads[:4]:
        copy.wait()
    store(down_v, down_hbm)
    store(up_v, up_hbm)
    for n in range(tiles):
        at = pl.ds(n * TILE, TILE)
        loads[4 + 2 * n].wait()
        grad_o[:, at] = dot(place_v[...], grad_v[:, at]).astype(BF)
        store(grad_o.at[:, at], grad_hbm.at[:, at])
        loads[5 + 2 * n].wait()
        looped_o[:, at] = dot(unplace_v[...], loop_v[:, at]).astype(BF)
        store(looped_o.at[:, at], looped_hbm.at[:, at])
    for copy in stores:
        copy.wait()


def fused_body(
    hidden, depths, packed_slot_index, value_weight, output_weight, adapter_down_factor,
    adapter_up_factor, before_norm_gain, after_norm_gain, cotangent,
):
    tok, width = hidden.shape
    act = cotangent.shape[0]
    n_dp, n_seq = lax.axis_size("dp"), lax.axis_size("seq")
    v_rows, value_width = value_weight.shape
    o_rows = output_weight.shape[0]
    rank = adapter_up_factor.shape[1]
    cols = rank // n_seq
    lead = -(-v_rows // 128) * 128 + o_rows
    vm, hbm = pl.BlockSpec(memory_space=pltpu.VMEM), pl.BlockSpec(memory_space=pltpu.HBM)
    dma = pltpu.SemaphoreType.DMA
    rows = n_seq * CAP

    def b16(*shape):
        return pltpu.VMEM(shape, BF)

    def f32(*shape):
        return pltpu.VMEM(shape, F32)

    sh = jax.ShapeDtypeStruct
    lora = (sh((cols, v_rows), F32), sh((cols, o_rows), F32))
    between = (
        sh((rows, width), BF), sh((rows, width), BF), sh((tok, rows), BF), sh((act, rows), BF),
    ) + lora
    early = n_seq * EARLY
    tiles = width // TILE
    results = pl.pallas_call(
        fused_kernel,
        out_shape=between,
        in_specs=[hbm] * 10,
        out_specs=(hbm,) * 6,
        scratch_shapes=[
            pltpu.VMEM((tok // 128, 128), jnp.int32),
            pltpu.VMEM((tok // 128, 128), jnp.int32),
            f32(width // 128, 128),
            f32(width // 128, 128),
            b16(tok, width),
            b16(act, width),
            b16(v_rows * n_dp, value_width + rank),
            b16(o_rows * n_dp, width),
            b16(o_rows * n_dp, rank),
            b16(rows, 128),
            b16(rows, 128),
            b16(rows, width),
            b16(rows, width),
            f32(1, width),
            f32(1, width),
            b16(rows, width),
            b16(rows, width),
            b16(rows, value_width),
            b16(rows, rank),
            f32(rows, width),
            b16(rows, width),
            b16(rows, value_width + rank),
            b16(rows, width),
            b16(tok, rows),
            b16(rows, tok),
            b16(rows, 128),
            b16(128, rows),
            b16(n_dp // 2, 2, rank, lead),
            b16(n_dp // 2, rank, lead),
            b16(n_dp // 2, rank, lead),
            b16(4, rank, lead),
            b16(rank, lead),
            b16(n_seq, cols, lead),
            f32(rows, 128),
            f32(rows, 128),
            f32(rows, 128),
            f32(early, 128),
            b16(early, width),
            b16(early, value_width),
            f32(early, width),
            b16(early, width),
            b16(rows, width),
            f32(cols, v_rows),
            f32(cols, o_rows),
        ]
        + [dma((n,)) for n in (42, 42, 8, 8) + (4,) * 10 + (8, 8, 4, 4, 10, 10)],
        compiler_params=pltpu.CompilerParams(
            collective_id=0, has_side_effects=True, vmem_limit_bytes=56 << 20
        ),
        name="layer",
    )(
        packed_slot_index.reshape(tok // 128, 128),
        depths.reshape(tok // 128, 128),
        before_norm_gain.reshape(width // 128, 128),
        after_norm_gain.reshape(width // 128, 128),
        hidden,
        cotangent,
        value_weight,
        output_weight,
        adapter_down_factor,
        adapter_up_factor,
    )
    looped, grad, down, up = pl.pallas_call(
        store_kernel,
        out_shape=(sh((act, width), BF), sh((tok, width), BF)) + lora,
        in_specs=[hbm] * 6,
        out_specs=(hbm,) * 4,
        scratch_shapes=[
            b16(rows, width),
            b16(rows, width),
            b16(tok, rows),
            b16(act, rows),
            f32(cols, v_rows),
            f32(cols, o_rows),
            b16(act, width),
            b16(tok, width),
            dma((4 + 2 * tiles,)),
            dma((2 + 2 * tiles,)),
        ],
        compiler_params=pltpu.CompilerParams(vmem_limit_bytes=56 << 20),
        name="store",
    )(*results)
    return looped, grad, down.T, up.T


def body(*arrays):
    fits = (
        lax.axis_size("dp") == 8
        and lax.axis_size("seq") == 4
        and arrays[0].shape[0] == 4 * CAP
        and arrays[9].shape[0] == 128
        and arrays[0].shape[1] % 256 == 0
        and arrays[3].shape[1] % 256 == 0
        and all(arrays[i].shape[0] % 32 == 0 for i in (3, 4, 5, 6))
        and arrays[4].shape[0] == 128
        and arrays[6].shape[1] == 128
    )
    return (fused_body if fits else general_body)(*arrays)


def solution(mesh):
    placed = (
        P(("dp", "seq"), None),
        P(("dp", "seq")),
        P(("dp", "seq")),
        P("dp", None),
        P("dp", None),
        P("dp", None),
        P("dp", None),
        P(),
        P(),
        P(("dp", "seq"), None),
    )
    return jax.shard_map(
        body,
        mesh=mesh,
        in_specs=placed,
        out_specs=(P(("dp", "seq"), None), P(("dp", "seq"), None), P("dp", "seq"), P("dp", "seq")),
        check_vma=False,
    )
```

```python
import functools
import math

import jax
import jax.numpy as jnp
from jax import lax
from jax.experimental import pallas as pl
from jax.experimental.pallas import tpu as pltpu
from jax.sharding import PartitionSpec as P

epsilon = 1e-06


def contract_final_axis(left, right):
    return lax.dot_general(
        left, right, (((1,), (1,)), ((), ())), preferred_element_type=jnp.float32
    )


def contract_first(left, right):
    return lax.dot_general(
        left, right, (((0,), (0,)), ((), ())), preferred_element_type=jnp.float32
    )


def layer_forward(
    input_rows,
    cotangent_rows,
    value_weight,
    output_weight,
    adapter_down_factor,
    adapter_up_factor,
    before_norm_gain,
    after_norm_gain,
):
    x_float = input_rows.astype(jnp.float32)
    inv_pre = lax.rsqrt(jnp.mean(x_float * x_float, axis=-1, keepdims=True) + epsilon)
    whitened = x_float * inv_pre
    normalized_rows = (whitened * before_norm_gain).astype(jnp.bfloat16)
    rank_reduced = jnp.dot(
        normalized_rows, adapter_down_factor, preferred_element_type=jnp.float32
    ).astype(jnp.bfloat16)
    projected_rows = (
        jnp.dot(normalized_rows, value_weight, preferred_element_type=jnp.float32)
        + contract_final_axis(rank_reduced, adapter_up_factor)
    ).astype(jnp.bfloat16)
    mixed_out = jnp.dot(projected_rows, output_weight, preferred_element_type=jnp.float32)
    inv_post = lax.rsqrt(jnp.mean(mixed_out * mixed_out, axis=-1, keepdims=True) + epsilon)
    shaped = mixed_out * inv_post
    looped = (x_float + shaped * after_norm_gain).astype(jnp.bfloat16)
    cot_float = cotangent_rows.astype(jnp.float32)
    grad_shaped = cot_float * after_norm_gain
    grad_mixed = (
        inv_post * (grad_shaped - shaped * jnp.mean(grad_shaped * shaped, axis=-1, keepdims=True))
    ).astype(jnp.bfloat16)
    value_gradient = contract_final_axis(grad_mixed, output_weight).astype(jnp.bfloat16)
    low_rank_gradient = jnp.dot(
        value_gradient, adapter_up_factor, preferred_element_type=jnp.float32
    ).astype(jnp.bfloat16)
    normalized_gradient = contract_final_axis(value_gradient, value_weight) + contract_final_axis(
        low_rank_gradient, adapter_down_factor
    )
    grad_white = normalized_gradient * before_norm_gain
    gradient_rows = (
        cot_float
        + inv_pre
        * (grad_white - whitened * jnp.mean(grad_white * whitened, axis=-1, keepdims=True))
    ).astype(jnp.bfloat16)
    down_factor_gradient = contract_first(normalized_rows, low_rank_gradient)
    up_factor_gradient = contract_first(value_gradient, rank_reduced)
    return (looped, gradient_rows, down_factor_gradient, up_factor_gradient)


def general_body(
    hidden,
    depths,
    packed_slot_index,
    value_weight,
    output_weight,
    adapter_down_factor,
    adapter_up_factor,
    before_norm_gain,
    after_norm_gain,
    cotangent,
):
    seq_count = lax.axis_size("seq")
    own_index = lax.axis_index("seq")
    tok_count = hidden.shape[0]
    act_rows = cotangent.shape[0]
    value_full, out_full, down_full, up_full = (
        lax.all_gather(value_weight, "dp", axis=0, tiled=True),
        lax.all_gather(output_weight, "dp", axis=0, tiled=True),
        lax.all_gather(adapter_down_factor, "dp", axis=0, tiled=True),
        lax.all_gather(adapter_up_factor, "dp", axis=0, tiled=True),
    )
    depth_all, slot_all = (
        lax.all_gather(depths, "seq", axis=0, tiled=True),
        lax.all_gather(packed_slot_index, "seq", axis=0, tiled=True),
    )
    active_all = depth_all >= 2
    dest_all = jnp.where(active_all, slot_all // act_rows, -1)
    pos_all = jnp.where(active_all, slot_all % act_rows, 0)
    mine = active_all & (dest_all == own_index)
    active = depths >= 2
    zero_row = jnp.zeros((), jnp.bfloat16)
    rows_all = lax.all_gather(hidden, "seq", axis=0, tiled=True)
    source = (
        jnp.zeros((act_rows,), jnp.int32)
        .at[jnp.where(mine, pos_all, act_rows)]
        .set(jnp.arange(seq_count * tok_count, dtype=jnp.int32), mode="drop")
    )
    packed = jnp.take(rows_all, source, axis=0)
    looped, gradient_rows, down_factor_gradient, up_factor_gradient = layer_forward(
        packed,
        cotangent,
        value_full,
        out_full,
        down_full,
        up_full,
        before_norm_gain,
        after_norm_gain,
    )
    grads_all = lax.all_gather(gradient_rows, "seq", axis=0, tiled=True)
    picked = jnp.take(grads_all, jnp.maximum(packed_slot_index, 0), axis=0)
    grad_hidden = jnp.where(active[:, None], picked, zero_row)
    grad_scale = 1.0 / math.sqrt(seq_count * act_rows * lax.axis_size("dp"))
    down_term = down_factor_gradient * grad_scale
    up_term = up_factor_gradient * grad_scale
    down_mid, up_mid = (
        lax.psum_scatter(
            down_term.astype(jnp.bfloat16), "seq", scatter_dimension=1, tiled=True
        ).astype(jnp.float32),
        lax.psum_scatter(
            up_term.astype(jnp.bfloat16), "seq", scatter_dimension=1, tiled=True
        ).astype(jnp.float32),
    )
    down_sum, up_sum = (
        lax.psum_scatter(down_mid, "dp", scatter_dimension=0, tiled=True),
        lax.psum_scatter(up_mid, "dp", scatter_dimension=0, tiled=True),
    )
    return (looped, grad_hidden, down_sum, up_sum)


MESH = pl.DeviceIdType.MESH
BF, F32 = jnp.bfloat16, jnp.float32
CAP = 64
TILE = 256
EARLY = 16
LATE = CAP - EARLY


def dot(left, right, left_axis=1, right_axis=0):
    return lax.dot_general(
        left, right, (((left_axis,), (right_axis,)), ((), ())), preferred_element_type=F32
    )


def fused_kernel(
    slot_hbm, depth_hbm, gain_b_hbm, gain_a_hbm, hidden_hbm, cot_hbm, wv_in, wo_in, dn_in, up_in,
    grad_hbm, loop_hbm, unplace_hbm, down_hbm, up_hbm,
    slot_v, depth_v, gain_b_v, gain_a_v, hid, cot, wvd, wo, up, psend, precv, csend, crecv,
    gain_b, gain_a, xs, normed, proj, low, mixed, gm, gvl, looped, place_t, place, unplace,
    unplace_t, lsend, lpair, lsum, lrecv, zsend, zrecv, stat_a, stat_b, stat_c, stat_e,
    hid_e, proj_e, mixed_e, looped_e, grad_v, down_v, up_v,
    w_send, w_recv, u_send, u_recv, p_send, p_recv, c_send, c_recv, o_send, o_recv,
    h_send, h_recv, q_send, q_recv, l_send, l_recv, z_send, z_recv, loc, fin,
):
    dp, seq = lax.axis_index("dp"), lax.axis_index("seq")
    n_dp, n_seq = 8, 4
    width = hid.shape[1]
    value_width = proj.shape[1]
    core, x, y = dp % 2, (dp // 2) % 2, dp // 4
    nbr_x, nbr_y, sib = dp + 2 - 4 * x, dp + 4 - 8 * y, dp + 1 - 2 * core
    diag = nbr_x + 4 - 8 * y
    to_sib = 1 - 2 * core
    odd = seq % 2
    seq_mate = seq + 1 - 2 * odd
    v_rows, o_rows = wv_in.shape[0], wo_in.shape[0]
    tiles = width // TILE

    def lanes(n, size=TILE):
        return pl.ds(pl.multiple_of(n * size, size), size)

    own_v = pl.ds(pl.multiple_of(dp * v_rows, 16), v_rows)
    own_o = pl.ds(pl.multiple_of(dp * o_rows, 16), o_rows)
    moves = [
        (slot_hbm, slot_v),
        (depth_hbm, depth_v),
        (wv_in, wvd.at[own_v, pl.ds(0, value_width)]),
        (dn_in, wvd.at[own_v, pl.ds(value_width, 128)]),
        (wo_in, wo.at[own_o, :]),
        (up_in, up.at[own_o, :]),
        (hidden_hbm, hid),
        (cot_hbm, cot),
        (gain_b_hbm, gain_b_v),
        (gain_a_hbm, gain_a_v),
    ]
    local = [pltpu.make_async_copy(a, b, loc.at[i]) for i, (a, b) in enumerate(moves)]
    for copy in local:
        copy.start()

    barrier = pltpu.get_barrier_semaphore()
    for k in range(1, n_dp):
        pl.semaphore_signal(barrier, inc=1, device_id=((dp + k) % n_dp, seq), device_id_type=MESH)
    for k in range(1, n_seq):
        pl.semaphore_signal(barrier, inc=1, device_id=(dp, (seq + k) % n_seq), device_id_type=MESH)

    local[0].wait()
    local[1].wait()
    tok = hid.shape[0]
    rows = n_seq * CAP
    slots = jnp.concatenate([slot_v[i : i + 1, :] for i in range(tok // 128)], axis=1)
    depth = jnp.concatenate([depth_v[i : i + 1, :] for i in range(tok // 128)], axis=1)
    act = depth >= 2
    dest = jnp.where(act, slots // 128, -1)
    where_to = lax.broadcasted_iota(jnp.int32, (8, tok), 0) == dest
    earlier = (
        lax.broadcasted_iota(jnp.int32, (tok, tok), 0)
        < lax.broadcasted_iota(jnp.int32, (tok, tok), 1)
    ).astype(F32).astype(BF)
    counts = dot(where_to.astype(F32).astype(BF), earlier)
    rank = jnp.sum(jnp.where(where_to, counts, 0.0), axis=0, keepdims=True)
    row_of = jnp.where(act, dest.astype(F32) * CAP + rank, -1.0)
    picked = (lax.broadcasted_iota(jnp.int32, (rows, tok), 0).astype(F32) == row_of).astype(F32)
    position = jnp.where(act, slots - dest * 128 + 1, 0).astype(F32)
    pos_col = jnp.sum(picked * position, axis=1, keepdims=True) - 1.0
    psend[...] = jnp.broadcast_to(pos_col, (rows, 128)).astype(BF)
    for copy in local[2:6]:
        copy.wait()

    pl.semaphore_wait(barrier, n_dp - 1 + n_seq - 1)

    pending = []

    def block(owner, size=CAP):
        return pl.ds(pl.multiple_of(owner * size, 16), size)

    peers = (seq_mate, (seq + 2) % n_seq, n_seq - 1 - seq)

    def row_copy(src_buf, dst_buf, sends, recvs, k, first=0, count=CAP, stride=CAP):
        return pltpu.make_async_remote_copy(
            src_ref=src_buf.at[pl.ds(pl.multiple_of(peers[k] * CAP + first, 16), count), :],
            dst_ref=dst_buf.at[pl.ds(pl.multiple_of(seq * stride, 16), count), :],
            send_sem=sends.at[k], recv_sem=recvs.at[k], device_id=(dp, peers[k]),
            device_id_type=MESH,
        )

    def exchange(*args, order=(1, 2, 0), **kw):
        for k in order:
            copy = row_copy(*args, k, **kw)
            copy.start()
            pending.append(copy)

    def arrive(dst_buf, sends, recvs, count=CAP, stride=CAP, order=(0, 1, 2)):
        for k in order:
            here = dst_buf.at[pl.ds(pl.multiple_of(peers[k] * stride, 16), count), :]
            pltpu.make_async_remote_copy(
                src_ref=here, dst_ref=here, send_sem=sends.at[k], recv_sem=recvs.at[k],
                device_id=(dp, peers[k]), device_id_type=MESH,
            ).wait_recv()

    exchange(psend, precv, p_send, p_recv)
    precv[block(seq), :] = psend[block(seq), :]

    arrays = ((wvd, v_rows), (wo, o_rows))

    def region(a, owner, kind):
        full, size = arrays[a]
        half = size // 2
        first = -(-half // 32) * 16
        start, count = {
            "all": (0, size),
            "a": (odd * half, first),
            "b": (odd * half + first, half - first),
            "o": ((1 - odd) * half, half),
            "a2": ((1 - odd) * half, first),
            "b2": ((1 - odd) * half + first, half - first),
        }[kind]
        return full.at[pl.ds(pl.multiple_of(owner * size + start, 16), count), :]

    def piece(a, number, owner, kind, target):
        here = region(a, owner, kind)
        return pltpu.make_async_remote_copy(
            src_ref=here, dst_ref=here, send_sem=w_send.at[a * 21 + number],
            recv_sem=w_recv.at[a * 21 + number], device_id=target, device_id_type=MESH,
        )

    on_x, on_y, on_sib, on_z = (nbr_x, seq), (nbr_y, seq), (sib, seq), (dp, seq_mate)

    def send(*args):
        copy = piece(*args)
        copy.start()
        pending.append(copy)

    def got(a, number, owner, kind):
        piece(a, number, owner, kind, on_sib).wait_recv()

    def own_first(a):
        send(a, 0, dp, "a", on_x)
        send(a, 3, dp, "b", on_y)

    def own_second(a):
        send(a, 1, dp, "b", on_x)
        send(a, 4, dp, "a", on_y)

    def own_third(a):
        send(a, 2, dp, "o", on_x)
        send(a, 5, dp, "o", on_y)

    def forward_first(a):
        got(a, 0, nbr_x, "a")
        send(a, 7, nbr_x, "a", on_y)
        send(a, 9, nbr_x, "a", on_sib)
        got(a, 3, nbr_y, "b")
        send(a, 8, nbr_y, "b", on_x)
        send(a, 12, nbr_y, "b", on_sib)

    def forward_second(a):
        got(a, 1, nbr_x, "b")
        send(a, 10, nbr_x, "b", on_sib)
        got(a, 4, nbr_y, "a")
        send(a, 13, nbr_y, "a", on_sib)

    def forward_diag(a):
        got(a, 7, diag, "a")
        send(a, 15, diag, "a", on_z)
        send(a, 17, diag, "a", on_sib)
        got(a, 8, diag, "b")
        send(a, 16, diag, "b", on_z)
        send(a, 18, diag, "b", on_sib)

    def forward_third(a):
        got(a, 2, nbr_x, "o")
        send(a, 11, nbr_x, "o", on_sib)
        got(a, 5, nbr_y, "o")
        send(a, 14, nbr_y, "o", on_sib)

    def forward_last(a):
        got(a, 15, diag, "a2")
        send(a, 19, diag, "a2", on_sib)
        got(a, 16, diag, "b2")
        send(a, 20, diag, "b2", on_sib)

    def finish_x(a):
        got(a, 9, nbr_x + to_sib, "a")
        got(a, 10, nbr_x + to_sib, "b")
        got(a, 11, nbr_x + to_sib, "o")

    def finish_y(a):
        got(a, 12, nbr_y + to_sib, "b")
        got(a, 13, nbr_y + to_sib, "a")
        got(a, 14, nbr_y + to_sib, "o")

    def finish_diag(a):
        got(a, 17, diag + to_sib, "a")
        got(a, 18, diag + to_sib, "b")
        got(a, 19, diag + to_sib, "a2")
        got(a, 20, diag + to_sib, "b2")

    def up_copy(number, owner, target):
        here = up.at[pl.ds(pl.multiple_of(owner * o_rows, 16), o_rows), :]
        return pltpu.make_async_remote_copy(
            src_ref=here, dst_ref=here, send_sem=u_send.at[number], recv_sem=u_recv.at[number],
            device_id=target, device_id_type=MESH,
        )

    def up_send(number, owner, target):
        copy = up_copy(number, owner, target)
        copy.start()
        pending.append(copy)

    own_first(0)
    up_send(0, dp, on_x)
    up_send(1, dp, on_y)
    up_send(2, dp, (diag, seq))
    up_send(3, dp, on_sib)
    own_first(1)
    own_second(0)
    send(0, 6, dp, "all", on_sib)
    send(1, 6, dp, "all", on_sib)

    place[...] = picked.astype(BF)
    place_t[...] = picked.T.astype(BF)
    for copy in local[6:]:
        copy.wait()
    for i in range(width // 128):
        gain_b[:, i * 128 : (i + 1) * 128] = gain_b_v[i : i + 1, :]
        gain_a[:, i * 128 : (i + 1) * 128] = gain_a_v[i : i + 1, :]

    def fold(v):
        return v[:, :128] + v[:, 128:]

    def spread(v):
        return jnp.broadcast_to(v, (rows, 128))

    def wide(v):
        return jnp.concatenate([v, v], axis=1)

    arrive(precv, p_send, p_recv)
    at_lane = lax.broadcasted_iota(jnp.int32, (rows, 128), 1).astype(F32)
    chosen = (precv[...].astype(F32) == at_lane).astype(F32)
    unplace[...] = chosen.astype(BF)

    @pl.loop(0, tiles, unroll=True)
    def _(n):
        csend[:, lanes(n)] = dot(unplace[...], cot[:, lanes(n)]).astype(BF)

    cot_copies = [row_copy(csend, crecv, c_send, c_recv, k) for k in range(3)]
    pending.extend(cot_copies)
    inner = (seq == 1) | (seq == 2)

    @pl.when(jnp.logical_not(inner))
    def _():
        cot_copies[1].start()
        cot_copies[2].start()

    crecv[block(seq), :] = csend[block(seq), :]
    unplace_t[...] = chosen.T.astype(BF)
    saved = [
        pltpu.make_async_copy(unplace_t, unplace_hbm, fin.at[1]),
    ]
    for copy in saved:
        copy.start()

    stat_a[...] = jnp.zeros_like(stat_a)

    @pl.loop(0, tiles, unroll=True)
    def _(n):
        v = dot(place[...], hid[:, lanes(n)])
        xs[:, lanes(n)] = v.astype(BF)
        stat_a[...] += fold(v * v)

    inv_pre = lax.rsqrt(jnp.sum(stat_a[...], axis=1, keepdims=True) / width + epsilon)
    stat_a[...] = spread(inv_pre)

    @pl.loop(0, tiles, unroll=True)
    def _(n):
        v = xs[:, lanes(n)].astype(F32) * wide(stat_a[...])
        normed[:, lanes(n)] = (v * gain_b[:, lanes(n)]).astype(BF)

    forward_first(0)
    own_third(0)
    forward_first(1)
    own_second(1)
    own_third(1)
    for k, owner in enumerate((nbr_x, nbr_y, diag)):
        up_copy(k, owner, on_sib).wait_recv()
        up_send(4 + k, owner, on_sib)
    forward_second(0)

    forward_diag(0)

    @pl.when(inner)
    def _():
        cot_copies[1].start()
        cot_copies[2].start()

    forward_third(0)
    forward_diag(1)
    cot_copies[0].start()
    forward_last(0)
    got(0, 6, sib, "all")
    finish_x(0)
    finish_y(0)
    finish_diag(0)

    low[...] = dot(normed[...], wvd[:, value_width:]).astype(BF)
    up_copy(3, sib, on_sib).wait_recv()
    for k, owner in enumerate((nbr_x, nbr_y, diag)):
        up_copy(4 + k, owner + to_sib, on_sib).wait_recv()

    @pl.loop(0, value_width // TILE, unroll=True)
    def _(n):
        proj[:, lanes(n)] = (
            dot(normed[...], wvd[:, lanes(n)]) + dot(low[...], up[lanes(n), :], 1, 1)
        ).astype(BF)

    exchange(xs, hid_e, h_send, h_recv, first=LATE, count=EARLY, stride=EARLY, order=(1, 2))
    own_early = pl.ds(pl.multiple_of(seq * CAP + LATE, 16), EARLY)
    hid_e[block(seq, EARLY), :] = xs[own_early, :]
    hid_e[block(seq_mate, EARLY), :] = xs[own_early, :]
    exchange(proj, proj_e, q_send, q_recv, first=LATE, count=EARLY, stride=EARLY, order=(1, 2))
    proj_e[block(seq, EARLY), :] = proj[own_early, :]
    proj_e[block(seq_mate, EARLY), :] = proj[own_early, :]

    def mix(member, init=False, last=False):
        at = pl.ds(pl.multiple_of(member // 2 * 2 * o_rows, 256), 2 * o_rows)

        @pl.loop(0, tiles, unroll=True)
        def _(n):
            m = dot(proj[:, at], wo[at, lanes(n)])
            if not init:
                m += mixed[:, lanes(n)]
            mixed[:, lanes(n)] = m
            if last:
                stat_b[...] += fold(m * m)

    stat_b[...] = jnp.zeros_like(stat_b)
    got(1, 6, sib, "all")
    mix(dp, init=True)
    forward_second(1)
    forward_last(1)
    forward_third(1)
    finish_diag(1)
    mix(diag)
    finish_x(1)
    mix(nbr_x)
    finish_y(1)
    mix(nbr_y, last=True)

    inv_post = lax.rsqrt(jnp.sum(stat_b[...], axis=1, keepdims=True) / width + epsilon)
    stat_b[...] = spread(inv_post)

    @pl.loop(0, tiles, unroll=True)
    def _(n):
        shaped = mixed[:, lanes(n)] * wide(stat_b[...])
        v = xs[:, lanes(n)].astype(F32) + shaped * gain_a[:, lanes(n)]
        looped[:, lanes(n)] = v.astype(BF)

    exchange(looped, loop_hbm, o_send, o_recv, count=LATE, order=(1, 2))
    exchange(looped, loop_hbm, o_send, o_recv, order=(0,))
    saved.append(
        pltpu.make_async_copy(
            looped.at[block(seq), :],
            loop_hbm.at[block(seq), :],
            fin.at[2],
        )
    )
    saved[-1].start()
    arrive(crecv, c_send, c_recv)
    stat_c[...] = jnp.zeros_like(stat_c)

    @pl.loop(0, tiles, unroll=True)
    def _(n):
        g = crecv[:, lanes(n)].astype(F32) * gain_a[:, lanes(n)]
        stat_c[...] += fold(g * (mixed[:, lanes(n)] * wide(stat_b[...])))

    pull = jnp.sum(stat_c[...], axis=1, keepdims=True) / width
    stat_c[...] = spread(pull)

    @pl.loop(0, tiles, unroll=True)
    def _(n):
        g = crecv[:, lanes(n)].astype(F32) * gain_a[:, lanes(n)]
        inv = wide(stat_b[...])
        shaped = mixed[:, lanes(n)] * inv
        gm[:, lanes(n)] = (inv * (g - shaped * wide(stat_c[...]))).astype(BF)

    @pl.loop(0, value_width // TILE, unroll=True)
    def _(n):
        gvl[:, lanes(n)] = dot(gm[...], wo[lanes(n), :], 1, 1).astype(BF)

    grad_low = dot(gvl[:, :value_width], up[...]).astype(BF)
    gvl[:, value_width:] = grad_low

    down_term = dot(grad_low, normed[...], 0, 0).astype(BF)
    up_term = dot(low[...], gvl[:, :value_width], 0, 0).astype(BF)
    spare = jnp.zeros((128, lsend.shape[3] - v_rows - o_rows), BF)
    for owner in range(n_dp):
        lsend[owner // 2, owner % 2] = jnp.concatenate(
            [
                down_term[:, owner * v_rows : (owner + 1) * v_rows],
                spare,
                up_term[:, owner * o_rows : (owner + 1) * o_rows],
            ],
            axis=1,
        )
    pair = pltpu.make_async_remote_copy(
        src_ref=lsend.at[:, 1 - core], dst_ref=lpair, send_sem=l_send.at[0],
        recv_sem=l_recv.at[0], device_id=on_sib, device_id_type=MESH,
    )
    pair.start()
    pending.append(pair)

    stat_c[...] = jnp.zeros_like(stat_c)

    @pl.loop(0, tiles, unroll=True)
    def _(n):
        g = dot(gvl[...], wvd[lanes(n), :], 1, 1) * gain_b[:, lanes(n)]
        mixed[:, lanes(n)] = g
        stat_c[...] += fold(g * (xs[:, lanes(n)].astype(F32) * wide(stat_a[...])))

    pair.wait_recv()
    lsum[...] = (lsend[:, core].astype(F32) + lpair[...].astype(F32)).astype(BF)
    chip = dp // 2
    for k, target in ((1, nbr_x), (2, nbr_y), (3, diag)):
        copy = pltpu.make_async_remote_copy(
            src_ref=lsum.at[target // 2], dst_ref=lrecv.at[k], send_sem=l_send.at[k],
            recv_sem=l_recv.at[k], device_id=(target, seq), device_id_type=MESH,
        )
        copy.start()
        pending.append(copy)

    pull = jnp.sum(stat_c[...], axis=1, keepdims=True) / width
    stat_c[...] = spread(pull)

    @pl.loop(0, tiles, unroll=True)
    def _(n):
        inv = wide(stat_a[...])
        whitened = xs[:, lanes(n)].astype(F32) * inv
        g = crecv[:, lanes(n)].astype(F32) + inv * (
            mixed[:, lanes(n)] - whitened * wide(stat_c[...])
        )
        grad_v[:, lanes(n)] = dot(place_t[...], g.astype(BF)).astype(BF)

    saved.append(pltpu.make_async_copy(grad_v, grad_hbm, fin.at[3]))
    saved[-1].start()

    for k, origin in ((1, nbr_x), (2, nbr_y), (3, diag)):
        here = lrecv.at[k]
        pltpu.make_async_remote_copy(
            src_ref=here, dst_ref=here, send_sem=l_send.at[k], recv_sem=l_recv.at[k],
            device_id=(origin, seq), device_id_type=MESH,
        ).wait_recv()
    total = lsum[chip].astype(F32)
    for k in (1, 2, 3):
        total += lrecv[k].astype(F32)
    zsend[...] = total.astype(BF)
    cols = down_v.shape[0]
    for k in range(1, n_seq):
        target = (seq + k) % n_seq
        copy = pltpu.make_async_remote_copy(
            src_ref=zsend.at[block(target, cols), :], dst_ref=zrecv.at[seq],
            send_sem=z_send.at[k], recv_sem=z_recv.at[k], device_id=(dp, target),
            device_id_type=MESH,
        )
        copy.start()
        pending.append(copy)
    zrecv[seq] = zsend[block(seq, cols), :]

    arrive(hid_e, h_send, h_recv, count=EARLY, stride=EARLY, order=(1, 2))
    arrive(proj_e, q_send, q_recv, count=EARLY, stride=EARLY, order=(1, 2))
    stat_e[...] = jnp.zeros_like(stat_e)

    @pl.loop(0, tiles, unroll=True)
    def _(n):
        m = dot(proj_e[...], wo[:, lanes(n)])
        mixed_e[:, lanes(n)] = m
        stat_e[...] += fold(m * m)

    inv_early = lax.rsqrt(jnp.sum(stat_e[...], axis=1, keepdims=True) / width + epsilon)
    stat_e[...] = jnp.broadcast_to(inv_early, stat_e.shape)

    @pl.loop(0, tiles, unroll=True)
    def _(n):
        shaped = mixed_e[:, lanes(n)] * wide(stat_e[...])
        v = hid_e[:, lanes(n)].astype(F32) + shaped * gain_a[:, lanes(n)]
        looped_e[:, lanes(n)] = v.astype(BF)

    for i in (1, 2):
        saved.append(
            pltpu.make_async_copy(
                looped_e.at[block(peers[i], EARLY), :],
                loop_hbm.at[pl.ds(pl.multiple_of(peers[i] * CAP + LATE, 16), EARLY), :],
                fin.at[4 + i],
            )
        )
        saved[-1].start()

    for k in range(1, n_seq):
        origin = (seq + n_seq - k) % n_seq
        here = zrecv.at[origin]
        pltpu.make_async_remote_copy(
            src_ref=here, dst_ref=here, send_sem=z_send.at[k], recv_sem=z_recv.at[k],
            device_id=(dp, origin), device_id_type=MESH,
        ).wait_recv()
    grad_scale = 1.0 / math.sqrt(n_seq * cot.shape[0] * n_dp)
    part = [zrecv[i].astype(F32) for i in range(n_seq)]
    mine = ((part[0] + part[1]) + (part[2] + part[3])) * grad_scale
    down_v[...] = mine[:, :v_rows]
    up_v[...] = mine[:, lsend.shape[3] - o_rows :]
    saved.append(pltpu.make_async_copy(down_v, down_hbm, fin.at[8]))
    saved.append(pltpu.make_async_copy(up_v, up_hbm, fin.at[9]))
    saved[-2].start()
    saved[-1].start()

    arrive(loop_hbm, o_send, o_recv, count=LATE, order=(1, 2))
    arrive(loop_hbm, o_send, o_recv, order=(0,))
    for copy in pending:
        copy.wait_send()
    for copy in saved:
        copy.wait()


def store_kernel(
    grad_in, loop_in, unplace_in, down_in, up_in, looped_hbm, grad_hbm, down_hbm, up_hbm,
    grad_v, loop_v, unplace_v, down_v, up_v, looped_o, ins, outs,
):
    moves = [
        (unplace_in, unplace_v, None),
        (loop_in, loop_v, None),
        (grad_in, grad_v, grad_hbm),
        (down_in, down_v, down_hbm),
        (up_in, up_v, up_hbm),
    ]
    loads = [pltpu.make_async_copy(a, b, ins.at[i]) for i, (a, b, _) in enumerate(moves)]
    for copy in loads:
        copy.start()
    stores = [pltpu.make_async_copy(moves[i][1], moves[i][2], outs.at[i]) for i in (2, 3, 4)]
    loads[0].wait()
    loads[1].wait()
    width = loop_v.shape[1]
    half = width // 2
    for k in range(2):
        at = pl.ds(k * half, half)
        looped_o[:, at] = dot(unplace_v[...], loop_v[:, at]).astype(BF)
        stores.append(
            pltpu.make_async_copy(looped_o.at[:, at], looped_hbm.at[:, at], outs.at[k])
        )
        stores[-1].start()
        if k == 0:
            for i in (2, 3, 4):
                loads[i].wait()
                stores[i - 2].start()
    for copy in stores:
        copy.wait()


def fused_body(
    hidden, depths, packed_slot_index, value_weight, output_weight, adapter_down_factor,
    adapter_up_factor, before_norm_gain, after_norm_gain, cotangent,
):
    tok, width = hidden.shape
    act = cotangent.shape[0]
    n_dp, n_seq = lax.axis_size("dp"), lax.axis_size("seq")
    v_rows, value_width = value_weight.shape
    o_rows = output_weight.shape[0]
    rank = adapter_up_factor.shape[1]
    cols = rank // n_seq
    lead = -(-v_rows // 128) * 128 + o_rows
    vm, hbm = pl.BlockSpec(memory_space=pltpu.VMEM), pl.BlockSpec(memory_space=pltpu.HBM)
    dma = pltpu.SemaphoreType.DMA
    rows = n_seq * CAP

    def b16(*shape):
        return pltpu.VMEM(shape, BF)

    def f32(*shape):
        return pltpu.VMEM(shape, F32)

    sh = jax.ShapeDtypeStruct
    lora = (sh((cols, v_rows), F32), sh((cols, o_rows), F32))
    between = (
        sh((tok, width), BF), sh((rows, width), BF), sh((act, rows), BF),
    ) + lora
    early = n_seq * EARLY
    results = pl.pallas_call(
        fused_kernel,
        out_shape=between,
        in_specs=[hbm] * 10,
        out_specs=(hbm,) * 5,
        scratch_shapes=[
            pltpu.VMEM((tok // 128, 128), jnp.int32),
            pltpu.VMEM((tok // 128, 128), jnp.int32),
            f32(width // 128, 128),
            f32(width // 128, 128),
            b16(tok, width),
            b16(act, width),
            b16(v_rows * n_dp, value_width + rank),
            b16(o_rows * n_dp, width),
            b16(o_rows * n_dp, rank),
            b16(rows, 128),
            b16(rows, 128),
            b16(rows, width),
            b16(rows, width),
            f32(1, width),
            f32(1, width),
            b16(rows, width),
            b16(rows, width),
            b16(rows, value_width),
            b16(rows, rank),
            f32(rows, width),
            b16(rows, width),
            b16(rows, value_width + rank),
            b16(rows, width),
            b16(tok, rows),
            b16(rows, tok),
            b16(rows, 128),
            b16(128, rows),
            b16(n_dp // 2, 2, rank, lead),
            b16(n_dp // 2, rank, lead),
            b16(n_dp // 2, rank, lead),
            b16(4, rank, lead),
            b16(rank, lead),
            b16(n_seq, cols, lead),
            f32(rows, 128),
            f32(rows, 128),
            f32(rows, 128),
            f32(early, 128),
            b16(early, width),
            b16(early, value_width),
            f32(early, width),
            b16(early, width),
            b16(rows, width),
            f32(cols, v_rows),
            f32(cols, o_rows),
        ]
        + [dma((n,)) for n in (42, 42, 8, 8) + (4,) * 10 + (8, 8, 4, 4, 10, 10)],
        compiler_params=pltpu.CompilerParams(
            collective_id=0, has_side_effects=True, vmem_limit_bytes=56 << 20
        ),
        name="layer",
    )(
        packed_slot_index.reshape(tok // 128, 128),
        depths.reshape(tok // 128, 128),
        before_norm_gain.reshape(width // 128, 128),
        after_norm_gain.reshape(width // 128, 128),
        hidden,
        cotangent,
        value_weight,
        output_weight,
        adapter_down_factor,
        adapter_up_factor,
    )
    looped, grad, down, up = pl.pallas_call(
        store_kernel,
        out_shape=(sh((act, width), BF), sh((tok, width), BF)) + lora,
        in_specs=[hbm] * 5,
        out_specs=(hbm,) * 4,
        scratch_shapes=[
            b16(tok, width),
            b16(rows, width),
            b16(act, rows),
            f32(cols, v_rows),
            f32(cols, o_rows),
            b16(act, width),
            dma((5,)),
            dma((5,)),
        ],
        compiler_params=pltpu.CompilerParams(vmem_limit_bytes=56 << 20),
        name="store",
    )(*results)
    return looped, grad, down.T, up.T


def body(*arrays):
    fits = (
        lax.axis_size("dp") == 8
        and lax.axis_size("seq") == 4
        and arrays[0].shape[0] == 4 * CAP
        and arrays[9].shape[0] == 128
        and arrays[0].shape[1] % 256 == 0
        and arrays[3].shape[1] % 256 == 0
        and all(arrays[i].shape[0] % 32 == 0 for i in (3, 4, 5, 6))
        and arrays[4].shape[0] == 128
        and arrays[6].shape[1] == 128
    )
    return (fused_body if fits else general_body)(*arrays)


def solution(mesh):
    placed = (
        P(("dp", "seq"), None),
        P(("dp", "seq")),
        P(("dp", "seq")),
        P("dp", None),
        P("dp", None),
        P("dp", None),
        P("dp", None),
        P(),
        P(),
        P(("dp", "seq"), None),
    )
    return jax.shard_map(
        body,
        mesh=mesh,
        in_specs=placed,
        out_specs=(P(("dp", "seq"), None), P(("dp", "seq"), None), P("dp", "seq"), P("dp", "seq")),
        check_vma=False,
    )
```

```python
import functools
import math

import jax
import jax.numpy as jnp
from jax import lax
from jax.experimental import pallas as pl
from jax.experimental.pallas import tpu as pltpu
from jax.sharding import PartitionSpec as P

epsilon = 1e-06


def contract_final_axis(left, right):
    return lax.dot_general(
        left, right, (((1,), (1,)), ((), ())), preferred_element_type=jnp.float32
    )


def contract_first(left, right):
    return lax.dot_general(
        left, right, (((0,), (0,)), ((), ())), preferred_element_type=jnp.float32
    )


def layer_forward(
    input_rows,
    cotangent_rows,
    value_weight,
    output_weight,
    adapter_down_factor,
    adapter_up_factor,
    before_norm_gain,
    after_norm_gain,
):
    x_float = input_rows.astype(jnp.float32)
    inv_pre = lax.rsqrt(jnp.mean(x_float * x_float, axis=-1, keepdims=True) + epsilon)
    whitened = x_float * inv_pre
    normalized_rows = (whitened * before_norm_gain).astype(jnp.bfloat16)
    rank_reduced = jnp.dot(
        normalized_rows, adapter_down_factor, preferred_element_type=jnp.float32
    ).astype(jnp.bfloat16)
    projected_rows = (
        jnp.dot(normalized_rows, value_weight, preferred_element_type=jnp.float32)
        + contract_final_axis(rank_reduced, adapter_up_factor)
    ).astype(jnp.bfloat16)
    mixed_out = jnp.dot(projected_rows, output_weight, preferred_element_type=jnp.float32)
    inv_post = lax.rsqrt(jnp.mean(mixed_out * mixed_out, axis=-1, keepdims=True) + epsilon)
    shaped = mixed_out * inv_post
    looped = (x_float + shaped * after_norm_gain).astype(jnp.bfloat16)
    cot_float = cotangent_rows.astype(jnp.float32)
    grad_shaped = cot_float * after_norm_gain
    grad_mixed = (
        inv_post * (grad_shaped - shaped * jnp.mean(grad_shaped * shaped, axis=-1, keepdims=True))
    ).astype(jnp.bfloat16)
    value_gradient = contract_final_axis(grad_mixed, output_weight).astype(jnp.bfloat16)
    low_rank_gradient = jnp.dot(
        value_gradient, adapter_up_factor, preferred_element_type=jnp.float32
    ).astype(jnp.bfloat16)
    normalized_gradient = contract_final_axis(value_gradient, value_weight) + contract_final_axis(
        low_rank_gradient, adapter_down_factor
    )
    grad_white = normalized_gradient * before_norm_gain
    gradient_rows = (
        cot_float
        + inv_pre
        * (grad_white - whitened * jnp.mean(grad_white * whitened, axis=-1, keepdims=True))
    ).astype(jnp.bfloat16)
    down_factor_gradient = contract_first(normalized_rows, low_rank_gradient)
    up_factor_gradient = contract_first(value_gradient, rank_reduced)
    return (looped, gradient_rows, down_factor_gradient, up_factor_gradient)


def general_body(
    hidden,
    depths,
    packed_slot_index,
    value_weight,
    output_weight,
    adapter_down_factor,
    adapter_up_factor,
    before_norm_gain,
    after_norm_gain,
    cotangent,
):
    seq_count = lax.axis_size("seq")
    own_index = lax.axis_index("seq")
    tok_count = hidden.shape[0]
    act_rows = cotangent.shape[0]
    value_full, out_full, down_full, up_full = (
        lax.all_gather(value_weight, "dp", axis=0, tiled=True),
        lax.all_gather(output_weight, "dp", axis=0, tiled=True),
        lax.all_gather(adapter_down_factor, "dp", axis=0, tiled=True),
        lax.all_gather(adapter_up_factor, "dp", axis=0, tiled=True),
    )
    depth_all, slot_all = (
        lax.all_gather(depths, "seq", axis=0, tiled=True),
        lax.all_gather(packed_slot_index, "seq", axis=0, tiled=True),
    )
    active_all = depth_all >= 2
    dest_all = jnp.where(active_all, slot_all // act_rows, -1)
    pos_all = jnp.where(active_all, slot_all % act_rows, 0)
    mine = active_all & (dest_all == own_index)
    active = depths >= 2
    zero_row = jnp.zeros((), jnp.bfloat16)
    rows_all = lax.all_gather(hidden, "seq", axis=0, tiled=True)
    source = (
        jnp.zeros((act_rows,), jnp.int32)
        .at[jnp.where(mine, pos_all, act_rows)]
        .set(jnp.arange(seq_count * tok_count, dtype=jnp.int32), mode="drop")
    )
    packed = jnp.take(rows_all, source, axis=0)
    looped, gradient_rows, down_factor_gradient, up_factor_gradient = layer_forward(
        packed,
        cotangent,
        value_full,
        out_full,
        down_full,
        up_full,
        before_norm_gain,
        after_norm_gain,
    )
    grads_all = lax.all_gather(gradient_rows, "seq", axis=0, tiled=True)
    picked = jnp.take(grads_all, jnp.maximum(packed_slot_index, 0), axis=0)
    grad_hidden = jnp.where(active[:, None], picked, zero_row)
    grad_scale = 1.0 / math.sqrt(seq_count * act_rows * lax.axis_size("dp"))
    down_term = down_factor_gradient * grad_scale
    up_term = up_factor_gradient * grad_scale
    down_mid, up_mid = (
        lax.psum_scatter(
            down_term.astype(jnp.bfloat16), "seq", scatter_dimension=1, tiled=True
        ).astype(jnp.float32),
        lax.psum_scatter(
            up_term.astype(jnp.bfloat16), "seq", scatter_dimension=1, tiled=True
        ).astype(jnp.float32),
    )
    down_sum, up_sum = (
        lax.psum_scatter(down_mid, "dp", scatter_dimension=0, tiled=True),
        lax.psum_scatter(up_mid, "dp", scatter_dimension=0, tiled=True),
    )
    return (looped, grad_hidden, down_sum, up_sum)


MESH = pl.DeviceIdType.MESH
BF, F32 = jnp.bfloat16, jnp.float32
CAP = 64
TILE = 256
EARLY = 16
LATE = CAP - EARLY


def dot(left, right, left_axis=1, right_axis=0):
    return lax.dot_general(
        left, right, (((left_axis,), (right_axis,)), ((), ())), preferred_element_type=F32
    )


def fused_kernel(
    slot_hbm, depth_hbm, gain_b_hbm, gain_a_hbm, hidden_hbm, cot_hbm, wv_in, wo_in, dn_in, up_in,
    grad_hbm, loop_hbm, unplace_hbm, down_hbm, up_hbm,
    slot_v, depth_v, gain_b_v, gain_a_v, hid, cot, wvd, wo, up, psend, precv, csend, crecv,
    gain_b, gain_a, xs, normed, proj, low, mixed, gm, gvl, looped, place_t, place, unplace,
    unplace_t, lsend, lpair, lsum, lrecv, zsend, zrecv, stat_a, stat_b, stat_c, stat_e,
    hid_e, proj_e, mixed_e, looped_e, grad_v, down_v, up_v,
    w_send, w_recv, u_send, u_recv, p_send, p_recv, c_send, c_recv, o_send, o_recv,
    h_send, h_recv, q_send, q_recv, l_send, l_recv, z_send, z_recv, loc, fin,
):
    dp, seq = lax.axis_index("dp"), lax.axis_index("seq")
    n_dp, n_seq = 8, 4
    width = hid.shape[1]
    value_width = proj.shape[1]
    core, x, y = dp % 2, (dp // 2) % 2, dp // 4
    nbr_x, nbr_y, sib = dp + 2 - 4 * x, dp + 4 - 8 * y, dp + 1 - 2 * core
    diag = nbr_x + 4 - 8 * y
    to_sib = 1 - 2 * core
    odd = seq % 2
    seq_mate = seq + 1 - 2 * odd
    v_rows, o_rows = wv_in.shape[0], wo_in.shape[0]
    tiles = width // TILE

    def lanes(n, size=TILE):
        return pl.ds(pl.multiple_of(n * size, size), size)

    own_v = pl.ds(pl.multiple_of(dp * v_rows, 16), v_rows)
    own_o = pl.ds(pl.multiple_of(dp * o_rows, 16), o_rows)
    moves = [
        (slot_hbm, slot_v),
        (depth_hbm, depth_v),
        (wv_in, wvd.at[own_v, pl.ds(0, value_width)]),
        (dn_in, wvd.at[own_v, pl.ds(value_width, 128)]),
        (wo_in, wo.at[own_o, :]),
        (up_in, up.at[own_o, :]),
        (hidden_hbm, hid),
        (cot_hbm, cot),
        (gain_b_hbm, gain_b_v),
        (gain_a_hbm, gain_a_v),
    ]
    local = [pltpu.make_async_copy(a, b, loc.at[i]) for i, (a, b) in enumerate(moves)]
    for copy in local:
        copy.start()

    barrier = pltpu.get_barrier_semaphore()
    for k in range(1, n_dp):
        pl.semaphore_signal(barrier, inc=1, device_id=((dp + k) % n_dp, seq), device_id_type=MESH)
    for k in range(1, n_seq):
        pl.semaphore_signal(barrier, inc=1, device_id=(dp, (seq + k) % n_seq), device_id_type=MESH)

    local[0].wait()
    local[1].wait()
    tok = hid.shape[0]
    rows = n_seq * CAP
    slots = jnp.concatenate([slot_v[i : i + 1, :] for i in range(tok // 128)], axis=1)
    depth = jnp.concatenate([depth_v[i : i + 1, :] for i in range(tok // 128)], axis=1)
    act = depth >= 2
    dest = jnp.where(act, slots // 128, -1)
    where_to = lax.broadcasted_iota(jnp.int32, (8, tok), 0) == dest
    earlier = (
        lax.broadcasted_iota(jnp.int32, (tok, tok), 0)
        < lax.broadcasted_iota(jnp.int32, (tok, tok), 1)
    ).astype(F32).astype(BF)
    counts = dot(where_to.astype(F32).astype(BF), earlier)
    rank = jnp.sum(jnp.where(where_to, counts, 0.0), axis=0, keepdims=True)
    row_of = jnp.where(act, dest.astype(F32) * CAP + rank, -1.0)
    picked = (lax.broadcasted_iota(jnp.int32, (rows, tok), 0).astype(F32) == row_of).astype(F32)
    position = jnp.where(act, slots - dest * 128 + 1, 0).astype(F32)
    pos_col = jnp.sum(picked * position, axis=1, keepdims=True) - 1.0
    psend[...] = jnp.broadcast_to(pos_col, (rows, 128)).astype(BF)
    for copy in local[2:6]:
        copy.wait()

    pl.semaphore_wait(barrier, n_dp - 1 + n_seq - 1)

    pending = []

    def block(owner, size=CAP):
        return pl.ds(pl.multiple_of(owner * size, 16), size)

    peers = (seq_mate, (seq + 2) % n_seq, n_seq - 1 - seq)

    def row_copy(src_buf, dst_buf, sends, recvs, k, first=0, count=CAP, stride=CAP):
        return pltpu.make_async_remote_copy(
            src_ref=src_buf.at[pl.ds(pl.multiple_of(peers[k] * CAP + first, 16), count), :],
            dst_ref=dst_buf.at[pl.ds(pl.multiple_of(seq * stride, 16), count), :],
            send_sem=sends.at[k], recv_sem=recvs.at[k], device_id=(dp, peers[k]),
            device_id_type=MESH,
        )

    def exchange(*args, order=(1, 2, 0), **kw):
        for k in order:
            copy = row_copy(*args, k, **kw)
            copy.start()
            pending.append(copy)

    def arrive(dst_buf, sends, recvs, count=CAP, stride=CAP, order=(0, 1, 2)):
        for k in order:
            here = dst_buf.at[pl.ds(pl.multiple_of(peers[k] * stride, 16), count), :]
            pltpu.make_async_remote_copy(
                src_ref=here, dst_ref=here, send_sem=sends.at[k], recv_sem=recvs.at[k],
                device_id=(dp, peers[k]), device_id_type=MESH,
            ).wait_recv()

    exchange(psend, precv, p_send, p_recv)
    precv[block(seq), :] = psend[block(seq), :]

    arrays = ((wvd, v_rows), (wo, o_rows))

    def region(a, owner, kind):
        full, size = arrays[a]
        half = size // 2
        first = -(-half // 32) * 16
        start, count = {
            "all": (0, size),
            "a": (odd * half, first),
            "b": (odd * half + first, half - first),
            "o": ((1 - odd) * half, half),
            "a2": ((1 - odd) * half, first),
            "b2": ((1 - odd) * half + first, half - first),
        }[kind]
        return full.at[pl.ds(pl.multiple_of(owner * size + start, 16), count), :]

    def piece(a, number, owner, kind, target):
        here = region(a, owner, kind)
        return pltpu.make_async_remote_copy(
            src_ref=here, dst_ref=here, send_sem=w_send.at[a * 21 + number],
            recv_sem=w_recv.at[a * 21 + number], device_id=target, device_id_type=MESH,
        )

    on_x, on_y, on_sib, on_z = (nbr_x, seq), (nbr_y, seq), (sib, seq), (dp, seq_mate)

    def send(*args):
        copy = piece(*args)
        copy.start()
        pending.append(copy)

    def got(a, number, owner, kind):
        piece(a, number, owner, kind, on_sib).wait_recv()

    def own_first(a):
        send(a, 0, dp, "a", on_x)
        send(a, 3, dp, "b", on_y)

    def own_second(a):
        send(a, 1, dp, "b", on_x)
        send(a, 4, dp, "a", on_y)

    def own_third(a):
        send(a, 2, dp, "o", on_x)
        send(a, 5, dp, "o", on_y)

    def forward_first(a):
        got(a, 0, nbr_x, "a")
        send(a, 7, nbr_x, "a", on_y)
        send(a, 9, nbr_x, "a", on_sib)
        got(a, 3, nbr_y, "b")
        send(a, 8, nbr_y, "b", on_x)
        send(a, 12, nbr_y, "b", on_sib)

    def forward_second(a):
        got(a, 1, nbr_x, "b")
        send(a, 10, nbr_x, "b", on_sib)
        got(a, 4, nbr_y, "a")
        send(a, 13, nbr_y, "a", on_sib)

    def forward_diag(a):
        got(a, 7, diag, "a")
        send(a, 15, diag, "a", on_z)
        send(a, 17, diag, "a", on_sib)
        got(a, 8, diag, "b")
        send(a, 16, diag, "b", on_z)
        send(a, 18, diag, "b", on_sib)

    def forward_third(a):
        got(a, 2, nbr_x, "o")
        send(a, 11, nbr_x, "o", on_sib)
        got(a, 5, nbr_y, "o")
        send(a, 14, nbr_y, "o", on_sib)

    def forward_last(a):
        got(a, 15, diag, "a2")
        send(a, 19, diag, "a2", on_sib)
        got(a, 16, diag, "b2")
        send(a, 20, diag, "b2", on_sib)

    def finish_x(a):
        got(a, 9, nbr_x + to_sib, "a")
        got(a, 10, nbr_x + to_sib, "b")
        got(a, 11, nbr_x + to_sib, "o")

    def finish_y(a):
        got(a, 12, nbr_y + to_sib, "b")
        got(a, 13, nbr_y + to_sib, "a")
        got(a, 14, nbr_y + to_sib, "o")

    def finish_diag(a):
        got(a, 17, diag + to_sib, "a")
        got(a, 18, diag + to_sib, "b")
        got(a, 19, diag + to_sib, "a2")
        got(a, 20, diag + to_sib, "b2")

    def up_copy(number, owner, target):
        here = up.at[pl.ds(pl.multiple_of(owner * o_rows, 16), o_rows), :]
        return pltpu.make_async_remote_copy(
            src_ref=here, dst_ref=here, send_sem=u_send.at[number], recv_sem=u_recv.at[number],
            device_id=target, device_id_type=MESH,
        )

    def up_send(number, owner, target):
        copy = up_copy(number, owner, target)
        copy.start()
        pending.append(copy)

    own_first(0)
    up_send(0, dp, on_x)
    up_send(1, dp, on_y)
    up_send(2, dp, (diag, seq))
    up_send(3, dp, on_sib)
    own_first(1)
    own_second(0)
    send(0, 6, dp, "all", on_sib)
    send(1, 6, dp, "all", on_sib)

    place[...] = picked.astype(BF)
    place_t[...] = picked.T.astype(BF)
    for copy in local[6:]:
        copy.wait()
    for i in range(width // 128):
        gain_b[:, i * 128 : (i + 1) * 128] = gain_b_v[i : i + 1, :]
        gain_a[:, i * 128 : (i + 1) * 128] = gain_a_v[i : i + 1, :]

    def fold(v):
        return v[:, :128] + v[:, 128:]

    def spread(v):
        return jnp.broadcast_to(v, (rows, 128))

    def wide(v):
        return jnp.concatenate([v, v], axis=1)

    arrive(precv, p_send, p_recv)
    at_lane = lax.broadcasted_iota(jnp.int32, (rows, 128), 1).astype(F32)
    chosen = (precv[...].astype(F32) == at_lane).astype(F32)
    unplace[...] = chosen.astype(BF)

    @pl.loop(0, tiles, unroll=True)
    def _(n):
        csend[:, lanes(n)] = dot(unplace[...], cot[:, lanes(n)]).astype(BF)

    cot_copies = [row_copy(csend, crecv, c_send, c_recv, k) for k in range(3)]
    pending.extend(cot_copies)
    inner = (seq == 1) | (seq == 2)

    @pl.when(jnp.logical_not(inner))
    def _():
        cot_copies[1].start()
        cot_copies[2].start()

    crecv[block(seq), :] = csend[block(seq), :]
    unplace_t[...] = chosen.T.astype(BF)
    saved = [
        pltpu.make_async_copy(unplace_t, unplace_hbm, fin.at[1]),
    ]
    for copy in saved:
        copy.start()

    stat_a[...] = jnp.zeros_like(stat_a)

    @pl.loop(0, tiles, unroll=True)
    def _(n):
        v = dot(place[...], hid[:, lanes(n)])
        xs[:, lanes(n)] = v.astype(BF)
        stat_a[...] += fold(v * v)

    inv_pre = lax.rsqrt(jnp.sum(stat_a[...], axis=1, keepdims=True) / width + epsilon)
    stat_a[...] = spread(inv_pre)

    @pl.loop(0, tiles, unroll=True)
    def _(n):
        v = xs[:, lanes(n)].astype(F32) * wide(stat_a[...])
        normed[:, lanes(n)] = (v * gain_b[:, lanes(n)]).astype(BF)

    forward_first(0)
    own_third(0)
    forward_first(1)
    own_second(1)
    own_third(1)
    for k, owner in enumerate((nbr_x, nbr_y, diag)):
        up_copy(k, owner, on_sib).wait_recv()
        up_send(4 + k, owner, on_sib)
    forward_second(0)

    forward_diag(0)

    @pl.when(inner)
    def _():
        cot_copies[1].start()
        cot_copies[2].start()

    forward_third(0)
    forward_diag(1)
    cot_copies[0].start()
    forward_last(0)
    got(0, 6, sib, "all")
    finish_x(0)
    finish_y(0)
    finish_diag(0)

    low[...] = dot(normed[...], wvd[:, value_width:]).astype(BF)
    up_copy(3, sib, on_sib).wait_recv()
    for k, owner in enumerate((nbr_x, nbr_y, diag)):
        up_copy(4 + k, owner + to_sib, on_sib).wait_recv()

    @pl.loop(0, value_width // TILE, unroll=True)
    def _(n):
        proj[:, lanes(n)] = (
            dot(normed[...], wvd[:, lanes(n)]) + dot(low[...], up[lanes(n), :], 1, 1)
        ).astype(BF)

    exchange(xs, hid_e, h_send, h_recv, first=LATE, count=EARLY, stride=EARLY, order=(1, 2))
    def mix(member, init=False, last=False):
        at = pl.ds(pl.multiple_of(member // 2 * 2 * o_rows, 256), 2 * o_rows)

        @pl.loop(0, tiles, unroll=True)
        def _(n):
            m = dot(proj[:, at], wo[at, lanes(n)])
            if not init:
                m += mixed[:, lanes(n)]
            mixed[:, lanes(n)] = m
            if last:
                stat_b[...] += fold(m * m)

    stat_b[...] = jnp.zeros_like(stat_b)
    got(1, 6, sib, "all")
    mix(dp, init=True)
    forward_second(1)
    forward_last(1)
    forward_third(1)
    own_early = pl.ds(pl.multiple_of(seq * CAP + LATE, 16), EARLY)
    hid_e[block(seq, EARLY), :] = xs[own_early, :]
    hid_e[block(seq_mate, EARLY), :] = xs[own_early, :]
    exchange(proj, proj_e, q_send, q_recv, first=LATE, count=EARLY, stride=EARLY, order=(1, 2))
    proj_e[block(seq, EARLY), :] = proj[own_early, :]
    proj_e[block(seq_mate, EARLY), :] = proj[own_early, :]
    finish_diag(1)
    mix(diag)
    finish_x(1)
    mix(nbr_x)
    finish_y(1)
    mix(nbr_y, last=True)

    inv_post = lax.rsqrt(jnp.sum(stat_b[...], axis=1, keepdims=True) / width + epsilon)
    stat_b[...] = spread(inv_post)

    @pl.loop(0, tiles, unroll=True)
    def _(n):
        shaped = mixed[:, lanes(n)] * wide(stat_b[...])
        v = xs[:, lanes(n)].astype(F32) + shaped * gain_a[:, lanes(n)]
        looped[:, lanes(n)] = v.astype(BF)

    exchange(looped, loop_hbm, o_send, o_recv, count=LATE, order=(1, 2))
    exchange(looped, loop_hbm, o_send, o_recv, order=(0,))
    saved.append(
        pltpu.make_async_copy(
            looped.at[block(seq), :],
            loop_hbm.at[block(seq), :],
            fin.at[2],
        )
    )
    saved[-1].start()
    arrive(crecv, c_send, c_recv)
    stat_c[...] = jnp.zeros_like(stat_c)

    @pl.loop(0, tiles, unroll=True)
    def _(n):
        g = crecv[:, lanes(n)].astype(F32) * gain_a[:, lanes(n)]
        stat_c[...] += fold(g * (mixed[:, lanes(n)] * wide(stat_b[...])))

    pull = jnp.sum(stat_c[...], axis=1, keepdims=True) / width
    stat_c[...] = spread(pull)

    @pl.loop(0, tiles, unroll=True)
    def _(n):
        g = crecv[:, lanes(n)].astype(F32) * gain_a[:, lanes(n)]
        inv = wide(stat_b[...])
        shaped = mixed[:, lanes(n)] * inv
        gm[:, lanes(n)] = (inv * (g - shaped * wide(stat_c[...]))).astype(BF)

    @pl.loop(0, value_width // TILE, unroll=True)
    def _(n):
        gvl[:, lanes(n)] = dot(gm[...], wo[lanes(n), :], 1, 1).astype(BF)

    grad_low = dot(gvl[:, :value_width], up[...]).astype(BF)
    gvl[:, value_width:] = grad_low

    down_term = dot(grad_low, normed[...], 0, 0).astype(BF)
    up_term = dot(low[...], gvl[:, :value_width], 0, 0).astype(BF)
    spare = jnp.zeros((128, lsend.shape[3] - v_rows - o_rows), BF)
    for owner in range(n_dp):
        lsend[owner // 2, owner % 2] = jnp.concatenate(
            [
                down_term[:, owner * v_rows : (owner + 1) * v_rows],
                spare,
                up_term[:, owner * o_rows : (owner + 1) * o_rows],
            ],
            axis=1,
        )
    pair = pltpu.make_async_remote_copy(
        src_ref=lsend.at[:, 1 - core], dst_ref=lpair, send_sem=l_send.at[0],
        recv_sem=l_recv.at[0], device_id=on_sib, device_id_type=MESH,
    )
    pair.start()
    pending.append(pair)

    pair.wait_recv()
    lsum[...] = (lsend[:, core].astype(F32) + lpair[...].astype(F32)).astype(BF)
    chip = dp // 2
    for k, target in ((1, nbr_x), (2, nbr_y), (3, diag)):
        copy = pltpu.make_async_remote_copy(
            src_ref=lsum.at[target // 2], dst_ref=lrecv.at[k], send_sem=l_send.at[k],
            recv_sem=l_recv.at[k], device_id=(target, seq), device_id_type=MESH,
        )
        copy.start()
        pending.append(copy)

    stat_c[...] = jnp.zeros_like(stat_c)

    @pl.loop(0, tiles, unroll=True)
    def _(n):
        g = dot(gvl[...], wvd[lanes(n), :], 1, 1) * gain_b[:, lanes(n)]
        mixed[:, lanes(n)] = g
        stat_c[...] += fold(g * (xs[:, lanes(n)].astype(F32) * wide(stat_a[...])))

    pull = jnp.sum(stat_c[...], axis=1, keepdims=True) / width
    stat_c[...] = spread(pull)

    @pl.loop(0, tiles, unroll=True)
    def _(n):
        inv = wide(stat_a[...])
        whitened = xs[:, lanes(n)].astype(F32) * inv
        g = crecv[:, lanes(n)].astype(F32) + inv * (
            mixed[:, lanes(n)] - whitened * wide(stat_c[...])
        )
        grad_v[:, lanes(n)] = dot(place_t[...], g.astype(BF)).astype(BF)

    saved.append(pltpu.make_async_copy(grad_v, grad_hbm, fin.at[3]))
    saved[-1].start()

    for k, origin in ((1, nbr_x), (2, nbr_y), (3, diag)):
        here = lrecv.at[k]
        pltpu.make_async_remote_copy(
            src_ref=here, dst_ref=here, send_sem=l_send.at[k], recv_sem=l_recv.at[k],
            device_id=(origin, seq), device_id_type=MESH,
        ).wait_recv()
    total = lsum[chip].astype(F32)
    for k in (1, 2, 3):
        total += lrecv[k].astype(F32)
    zsend[...] = total.astype(BF)
    cols = down_v.shape[0]
    for k in range(1, n_seq):
        target = (seq + k) % n_seq
        copy = pltpu.make_async_remote_copy(
            src_ref=zsend.at[block(target, cols), :], dst_ref=zrecv.at[seq],
            send_sem=z_send.at[k], recv_sem=z_recv.at[k], device_id=(dp, target),
            device_id_type=MESH,
        )
        copy.start()
        pending.append(copy)
    zrecv[seq] = zsend[block(seq, cols), :]

    arrive(hid_e, h_send, h_recv, count=EARLY, stride=EARLY, order=(1, 2))
    arrive(proj_e, q_send, q_recv, count=EARLY, stride=EARLY, order=(1, 2))
    stat_e[...] = jnp.zeros_like(stat_e)

    @pl.loop(0, tiles, unroll=True)
    def _(n):
        m = dot(proj_e[...], wo[:, lanes(n)])
        mixed_e[:, lanes(n)] = m
        stat_e[...] += fold(m * m)

    inv_early = lax.rsqrt(jnp.sum(stat_e[...], axis=1, keepdims=True) / width + epsilon)
    stat_e[...] = jnp.broadcast_to(inv_early, stat_e.shape)

    @pl.loop(0, tiles, unroll=True)
    def _(n):
        shaped = mixed_e[:, lanes(n)] * wide(stat_e[...])
        v = hid_e[:, lanes(n)].astype(F32) + shaped * gain_a[:, lanes(n)]
        looped_e[:, lanes(n)] = v.astype(BF)

    for i in (1, 2):
        saved.append(
            pltpu.make_async_copy(
                looped_e.at[block(peers[i], EARLY), :],
                loop_hbm.at[pl.ds(pl.multiple_of(peers[i] * CAP + LATE, 16), EARLY), :],
                fin.at[4 + i],
            )
        )
        saved[-1].start()

    for k in range(1, n_seq):
        origin = (seq + n_seq - k) % n_seq
        here = zrecv.at[origin]
        pltpu.make_async_remote_copy(
            src_ref=here, dst_ref=here, send_sem=z_send.at[k], recv_sem=z_recv.at[k],
            device_id=(dp, origin), device_id_type=MESH,
        ).wait_recv()
    grad_scale = 1.0 / math.sqrt(n_seq * cot.shape[0] * n_dp)
    part = [zrecv[i].astype(F32) for i in range(n_seq)]
    mine = ((part[0] + part[1]) + (part[2] + part[3])) * grad_scale
    down_v[...] = mine[:, :v_rows]
    up_v[...] = mine[:, lsend.shape[3] - o_rows :]
    saved.append(pltpu.make_async_copy(down_v, down_hbm, fin.at[8]))
    saved.append(pltpu.make_async_copy(up_v, up_hbm, fin.at[9]))
    saved[-2].start()
    saved[-1].start()

    arrive(loop_hbm, o_send, o_recv, count=LATE, order=(1, 2))
    arrive(loop_hbm, o_send, o_recv, order=(0,))
    for copy in pending:
        copy.wait_send()
    for copy in saved:
        copy.wait()


def store_kernel(
    grad_in, loop_in, unplace_in, down_in, up_in, looped_hbm, grad_hbm, down_hbm, up_hbm,
    grad_v, loop_v, unplace_v, down_v, up_v, looped_o, ins, outs,
):
    moves = [
        (unplace_in, unplace_v, None),
        (loop_in, loop_v, None),
        (grad_in, grad_v, grad_hbm),
        (down_in, down_v, down_hbm),
        (up_in, up_v, up_hbm),
    ]
    loads = [pltpu.make_async_copy(a, b, ins.at[i]) for i, (a, b, _) in enumerate(moves)]
    for copy in loads:
        copy.start()
    stores = [pltpu.make_async_copy(moves[i][1], moves[i][2], outs.at[i]) for i in (2, 3, 4)]
    loads[0].wait()
    loads[1].wait()
    width = loop_v.shape[1]
    half = width // 2
    for k in range(2):
        at = pl.ds(k * half, half)
        looped_o[:, at] = dot(unplace_v[...], loop_v[:, at]).astype(BF)
        stores.append(
            pltpu.make_async_copy(looped_o.at[:, at], looped_hbm.at[:, at], outs.at[k])
        )
        stores[-1].start()
        if k == 0:
            for i in (2, 3, 4):
                loads[i].wait()
                stores[i - 2].start()
    for copy in stores:
        copy.wait()


def fused_body(
    hidden, depths, packed_slot_index, value_weight, output_weight, adapter_down_factor,
    adapter_up_factor, before_norm_gain, after_norm_gain, cotangent,
):
    tok, width = hidden.shape
    act = cotangent.shape[0]
    n_dp, n_seq = lax.axis_size("dp"), lax.axis_size("seq")
    v_rows, value_width = value_weight.shape
    o_rows = output_weight.shape[0]
    rank = adapter_up_factor.shape[1]
    cols = rank // n_seq
    lead = -(-v_rows // 128) * 128 + o_rows
    vm, hbm = pl.BlockSpec(memory_space=pltpu.VMEM), pl.BlockSpec(memory_space=pltpu.HBM)
    dma = pltpu.SemaphoreType.DMA
    rows = n_seq * CAP

    def b16(*shape):
        return pltpu.VMEM(shape, BF)

    def f32(*shape):
        return pltpu.VMEM(shape, F32)

    sh = jax.ShapeDtypeStruct
    lora = (sh((cols, v_rows), F32), sh((cols, o_rows), F32))
    between = (
        sh((tok, width), BF), sh((rows, width), BF), sh((act, rows), BF),
    ) + lora
    early = n_seq * EARLY
    results = pl.pallas_call(
        fused_kernel,
        out_shape=between,
        in_specs=[hbm] * 10,
        out_specs=(hbm,) * 5,
        scratch_shapes=[
            pltpu.VMEM((tok // 128, 128), jnp.int32),
            pltpu.VMEM((tok // 128, 128), jnp.int32),
            f32(width // 128, 128),
            f32(width // 128, 128),
            b16(tok, width),
            b16(act, width),
            b16(v_rows * n_dp, value_width + rank),
            b16(o_rows * n_dp, width),
            b16(o_rows * n_dp, rank),
            b16(rows, 128),
            b16(rows, 128),
            b16(rows, width),
            b16(rows, width),
            f32(1, width),
            f32(1, width),
            b16(rows, width),
            b16(rows, width),
            b16(rows, value_width),
            b16(rows, rank),
            f32(rows, width),
            b16(rows, width),
            b16(rows, value_width + rank),
            b16(rows, width),
            b16(tok, rows),
            b16(rows, tok),
            b16(rows, 128),
            b16(128, rows),
            b16(n_dp // 2, 2, rank, lead),
            b16(n_dp // 2, rank, lead),
            b16(n_dp // 2, rank, lead),
            b16(4, rank, lead),
            b16(rank, lead),
            b16(n_seq, cols, lead),
            f32(rows, 128),
            f32(rows, 128),
            f32(rows, 128),
            f32(early, 128),
            b16(early, width),
            b16(early, value_width),
            f32(early, width),
            b16(early, width),
            b16(rows, width),
            f32(cols, v_rows),
            f32(cols, o_rows),
        ]
        + [dma((n,)) for n in (42, 42, 8, 8) + (4,) * 10 + (8, 8, 4, 4, 10, 10)],
        compiler_params=pltpu.CompilerParams(
            collective_id=0, has_side_effects=True, vmem_limit_bytes=56 << 20
        ),
        name="layer",
    )(
        packed_slot_index.reshape(tok // 128, 128),
        depths.reshape(tok // 128, 128),
        before_norm_gain.reshape(width // 128, 128),
        after_norm_gain.reshape(width // 128, 128),
        hidden,
        cotangent,
        value_weight,
        output_weight,
        adapter_down_factor,
        adapter_up_factor,
    )
    looped, grad, down, up = pl.pallas_call(
        store_kernel,
        out_shape=(sh((act, width), BF), sh((tok, width), BF)) + lora,
        in_specs=[hbm] * 5,
        out_specs=(hbm,) * 4,
        scratch_shapes=[
            b16(tok, width),
            b16(rows, width),
            b16(act, rows),
            f32(cols, v_rows),
            f32(cols, o_rows),
            b16(act, width),
            dma((5,)),
            dma((5,)),
        ],
        compiler_params=pltpu.CompilerParams(vmem_limit_bytes=56 << 20),
        name="store",
    )(*results)
    return looped, grad, down.T, up.T


def body(*arrays):
    fits = (
        lax.axis_size("dp") == 8
        and lax.axis_size("seq") == 4
        and arrays[0].shape[0] == 4 * CAP
        and arrays[9].shape[0] == 128
        and arrays[0].shape[1] % 256 == 0
        and arrays[3].shape[1] % 256 == 0
        and all(arrays[i].shape[0] % 32 == 0 for i in (3, 4, 5, 6))
        and arrays[4].shape[0] == 128
        and arrays[6].shape[1] == 128
    )
    return (fused_body if fits else general_body)(*arrays)


def solution(mesh):
    placed = (
        P(("dp", "seq"), None),
        P(("dp", "seq")),
        P(("dp", "seq")),
        P("dp", None),
        P("dp", None),
        P("dp", None),
        P("dp", None),
        P(),
        P(),
        P(("dp", "seq"), None),
    )
    return jax.shard_map(
        body,
        mesh=mesh,
        in_specs=placed,
        out_specs=(P(("dp", "seq"), None), P(("dp", "seq"), None), P("dp", "seq"), P("dp", "seq")),
        check_vma=False,
    )
```

```python
import functools
import math

import jax
import jax.numpy as jnp
from jax import lax
from jax.experimental import pallas as pl
from jax.experimental.pallas import tpu as pltpu
from jax.sharding import PartitionSpec as P

epsilon = 1e-06


def contract_final_axis(left, right):
    return lax.dot_general(
        left, right, (((1,), (1,)), ((), ())), preferred_element_type=jnp.float32
    )


def contract_first(left, right):
    return lax.dot_general(
        left, right, (((0,), (0,)), ((), ())), preferred_element_type=jnp.float32
    )


def layer_forward(
    input_rows,
    cotangent_rows,
    value_weight,
    output_weight,
    adapter_down_factor,
    adapter_up_factor,
    before_norm_gain,
    after_norm_gain,
):
    x_float = input_rows.astype(jnp.float32)
    inv_pre = lax.rsqrt(jnp.mean(x_float * x_float, axis=-1, keepdims=True) + epsilon)
    whitened = x_float * inv_pre
    normalized_rows = (whitened * before_norm_gain).astype(jnp.bfloat16)
    rank_reduced = jnp.dot(
        normalized_rows, adapter_down_factor, preferred_element_type=jnp.float32
    ).astype(jnp.bfloat16)
    projected_rows = (
        jnp.dot(normalized_rows, value_weight, preferred_element_type=jnp.float32)
        + contract_final_axis(rank_reduced, adapter_up_factor)
    ).astype(jnp.bfloat16)
    mixed_out = jnp.dot(projected_rows, output_weight, preferred_element_type=jnp.float32)
    inv_post = lax.rsqrt(jnp.mean(mixed_out * mixed_out, axis=-1, keepdims=True) + epsilon)
    shaped = mixed_out * inv_post
    looped = (x_float + shaped * after_norm_gain).astype(jnp.bfloat16)
    cot_float = cotangent_rows.astype(jnp.float32)
    grad_shaped = cot_float * after_norm_gain
    grad_mixed = (
        inv_post * (grad_shaped - shaped * jnp.mean(grad_shaped * shaped, axis=-1, keepdims=True))
    ).astype(jnp.bfloat16)
    value_gradient = contract_final_axis(grad_mixed, output_weight).astype(jnp.bfloat16)
    low_rank_gradient = jnp.dot(
        value_gradient, adapter_up_factor, preferred_element_type=jnp.float32
    ).astype(jnp.bfloat16)
    normalized_gradient = contract_final_axis(value_gradient, value_weight) + contract_final_axis(
        low_rank_gradient, adapter_down_factor
    )
    grad_white = normalized_gradient * before_norm_gain
    gradient_rows = (
        cot_float
        + inv_pre
        * (grad_white - whitened * jnp.mean(grad_white * whitened, axis=-1, keepdims=True))
    ).astype(jnp.bfloat16)
    down_factor_gradient = contract_first(normalized_rows, low_rank_gradient)
    up_factor_gradient = contract_first(value_gradient, rank_reduced)
    return (looped, gradient_rows, down_factor_gradient, up_factor_gradient)


def general_body(
    hidden,
    depths,
    packed_slot_index,
    value_weight,
    output_weight,
    adapter_down_factor,
    adapter_up_factor,
    before_norm_gain,
    after_norm_gain,
    cotangent,
):
    seq_count = lax.axis_size("seq")
    own_index = lax.axis_index("seq")
    tok_count = hidden.shape[0]
    act_rows = cotangent.shape[0]
    value_full, out_full, down_full, up_full = (
        lax.all_gather(value_weight, "dp", axis=0, tiled=True),
        lax.all_gather(output_weight, "dp", axis=0, tiled=True),
        lax.all_gather(adapter_down_factor, "dp", axis=0, tiled=True),
        lax.all_gather(adapter_up_factor, "dp", axis=0, tiled=True),
    )
    depth_all, slot_all = (
        lax.all_gather(depths, "seq", axis=0, tiled=True),
        lax.all_gather(packed_slot_index, "seq", axis=0, tiled=True),
    )
    active_all = depth_all >= 2
    dest_all = jnp.where(active_all, slot_all // act_rows, -1)
    pos_all = jnp.where(active_all, slot_all % act_rows, 0)
    mine = active_all & (dest_all == own_index)
    active = depths >= 2
    zero_row = jnp.zeros((), jnp.bfloat16)
    rows_all = lax.all_gather(hidden, "seq", axis=0, tiled=True)
    source = (
        jnp.zeros((act_rows,), jnp.int32)
        .at[jnp.where(mine, pos_all, act_rows)]
        .set(jnp.arange(seq_count * tok_count, dtype=jnp.int32), mode="drop")
    )
    packed = jnp.take(rows_all, source, axis=0)
    looped, gradient_rows, down_factor_gradient, up_factor_gradient = layer_forward(
        packed,
        cotangent,
        value_full,
        out_full,
        down_full,
        up_full,
        before_norm_gain,
        after_norm_gain,
    )
    grads_all = lax.all_gather(gradient_rows, "seq", axis=0, tiled=True)
    picked = jnp.take(grads_all, jnp.maximum(packed_slot_index, 0), axis=0)
    grad_hidden = jnp.where(active[:, None], picked, zero_row)
    grad_scale = 1.0 / math.sqrt(seq_count * act_rows * lax.axis_size("dp"))
    down_term = down_factor_gradient * grad_scale
    up_term = up_factor_gradient * grad_scale
    down_mid, up_mid = (
        lax.psum_scatter(
            down_term.astype(jnp.bfloat16), "seq", scatter_dimension=1, tiled=True
        ).astype(jnp.float32),
        lax.psum_scatter(
            up_term.astype(jnp.bfloat16), "seq", scatter_dimension=1, tiled=True
        ).astype(jnp.float32),
    )
    down_sum, up_sum = (
        lax.psum_scatter(down_mid, "dp", scatter_dimension=0, tiled=True),
        lax.psum_scatter(up_mid, "dp", scatter_dimension=0, tiled=True),
    )
    return (looped, grad_hidden, down_sum, up_sum)


MESH = pl.DeviceIdType.MESH
BF, F32 = jnp.bfloat16, jnp.float32
CAP = 64
TILE = 256
EARLY = 16
LATE = CAP - EARLY


def dot(left, right, left_axis=1, right_axis=0):
    return lax.dot_general(
        left, right, (((left_axis,), (right_axis,)), ((), ())), preferred_element_type=F32
    )


def fused_kernel(
    slot_hbm, depth_hbm, gain_b_hbm, gain_a_hbm, hidden_hbm, cot_hbm, wv_in, wo_in, dn_in, up_in,
    grad_hbm, loop_hbm, unplace_hbm, down_hbm, up_hbm,
    slot_v, depth_v, gain_b_v, gain_a_v, hid, cot, wvd, wo, up, psend, precv, csend, crecv,
    gain_b, gain_a, xs, normed, proj, low, mixed, gm, gvl, looped, place_t, place, unplace,
    unplace_t, lsend, lpair, lsum, lrecv, zsend, zrecv, stat_a, stat_b, stat_c, stat_e,
    hid_e, proj_e, mixed_e, looped_e, grad_v, down_v, up_v,
    w_send, w_recv, u_send, u_recv, p_send, p_recv, c_send, c_recv, o_send, o_recv,
    h_send, h_recv, q_send, q_recv, l_send, l_recv, z_send, z_recv, loc, fin,
):
    dp, seq = lax.axis_index("dp"), lax.axis_index("seq")
    n_dp, n_seq = 8, 4
    width = hid.shape[1]
    value_width = proj.shape[1]
    core, x, y = dp % 2, (dp // 2) % 2, dp // 4
    nbr_x, nbr_y, sib = dp + 2 - 4 * x, dp + 4 - 8 * y, dp + 1 - 2 * core
    diag = nbr_x + 4 - 8 * y
    to_sib = 1 - 2 * core
    odd = seq % 2
    seq_mate = seq + 1 - 2 * odd
    v_rows, o_rows = wv_in.shape[0], wo_in.shape[0]
    tiles = width // TILE

    def lanes(n, size=TILE):
        return pl.ds(pl.multiple_of(n * size, size), size)

    own_v = pl.ds(pl.multiple_of(dp * v_rows, 16), v_rows)
    own_o = pl.ds(pl.multiple_of(dp * o_rows, 16), o_rows)
    moves = [
        (slot_hbm, slot_v),
        (depth_hbm, depth_v),
        (wv_in, wvd.at[own_v, pl.ds(0, value_width)]),
        (dn_in, wvd.at[own_v, pl.ds(value_width, 128)]),
        (wo_in, wo.at[own_o, :]),
        (up_in, up.at[own_o, :]),
        (hidden_hbm, hid),
        (cot_hbm, cot),
        (gain_b_hbm, gain_b_v),
        (gain_a_hbm, gain_a_v),
    ]
    local = [pltpu.make_async_copy(a, b, loc.at[i]) for i, (a, b) in enumerate(moves)]
    for copy in local:
        copy.start()

    barrier = pltpu.get_barrier_semaphore()
    for k in range(1, n_dp):
        pl.semaphore_signal(barrier, inc=1, device_id=((dp + k) % n_dp, seq), device_id_type=MESH)
    for k in range(1, n_seq):
        pl.semaphore_signal(barrier, inc=1, device_id=(dp, (seq + k) % n_seq), device_id_type=MESH)

    local[0].wait()
    local[1].wait()
    tok = hid.shape[0]
    rows = n_seq * CAP
    slots = jnp.concatenate([slot_v[i : i + 1, :] for i in range(tok // 128)], axis=1)
    depth = jnp.concatenate([depth_v[i : i + 1, :] for i in range(tok // 128)], axis=1)
    act = depth >= 2
    dest = jnp.where(act, slots // 128, -1)
    where_to = lax.broadcasted_iota(jnp.int32, (8, tok), 0) == dest
    earlier = (
        lax.broadcasted_iota(jnp.int32, (tok, tok), 0)
        < lax.broadcasted_iota(jnp.int32, (tok, tok), 1)
    ).astype(F32).astype(BF)
    counts = dot(where_to.astype(F32).astype(BF), earlier)
    rank = jnp.sum(jnp.where(where_to, counts, 0.0), axis=0, keepdims=True)
    row_of = jnp.where(act, dest.astype(F32) * CAP + rank, -1.0)
    picked = (lax.broadcasted_iota(jnp.int32, (rows, tok), 0).astype(F32) == row_of).astype(F32)
    position = jnp.where(act, slots - dest * 128 + 1, 0).astype(F32)
    pos_col = jnp.sum(picked * position, axis=1, keepdims=True) - 1.0
    psend[...] = jnp.broadcast_to(pos_col, (rows, 128)).astype(BF)
    for copy in local[2:6]:
        copy.wait()

    pl.semaphore_wait(barrier, n_dp - 1 + n_seq - 1)

    pending = []

    def block(owner, size=CAP):
        return pl.ds(pl.multiple_of(owner * size, 16), size)

    peers = (seq_mate, (seq + 2) % n_seq, n_seq - 1 - seq)

    def row_copy(src_buf, dst_buf, sends, recvs, k, first=0, count=CAP, stride=CAP):
        return pltpu.make_async_remote_copy(
            src_ref=src_buf.at[pl.ds(pl.multiple_of(peers[k] * CAP + first, 16), count), :],
            dst_ref=dst_buf.at[pl.ds(pl.multiple_of(seq * stride, 16), count), :],
            send_sem=sends.at[k], recv_sem=recvs.at[k], device_id=(dp, peers[k]),
            device_id_type=MESH,
        )

    def exchange(*args, order=(1, 2, 0), **kw):
        for k in order:
            copy = row_copy(*args, k, **kw)
            copy.start()
            pending.append(copy)

    def arrive(dst_buf, sends, recvs, count=CAP, stride=CAP, order=(0, 1, 2)):
        for k in order:
            here = dst_buf.at[pl.ds(pl.multiple_of(peers[k] * stride, 16), count), :]
            pltpu.make_async_remote_copy(
                src_ref=here, dst_ref=here, send_sem=sends.at[k], recv_sem=recvs.at[k],
                device_id=(dp, peers[k]), device_id_type=MESH,
            ).wait_recv()

    exchange(psend, precv, p_send, p_recv)
    precv[block(seq), :] = psend[block(seq), :]

    arrays = ((wvd, v_rows), (wo, o_rows))

    def region(a, owner, kind):
        full, size = arrays[a]
        half = size // 2
        first = -(-half // 32) * 16
        start, count = {
            "all": (0, size),
            "a": (odd * half, first),
            "b": (odd * half + first, half - first),
            "o": ((1 - odd) * half, half),
            "a2": ((1 - odd) * half, first),
            "b2": ((1 - odd) * half + first, half - first),
        }[kind]
        return full.at[pl.ds(pl.multiple_of(owner * size + start, 16), count), :]

    def piece(a, number, owner, kind, target):
        here = region(a, owner, kind)
        return pltpu.make_async_remote_copy(
            src_ref=here, dst_ref=here, send_sem=w_send.at[a * 21 + number],
            recv_sem=w_recv.at[a * 21 + number], device_id=target, device_id_type=MESH,
        )

    on_x, on_y, on_sib, on_z = (nbr_x, seq), (nbr_y, seq), (sib, seq), (dp, seq_mate)

    def send(*args):
        copy = piece(*args)
        copy.start()
        pending.append(copy)

    def got(a, number, owner, kind):
        piece(a, number, owner, kind, on_sib).wait_recv()

    def own_first(a):
        send(a, 0, dp, "a", on_x)
        send(a, 3, dp, "b", on_y)

    def own_second(a):
        send(a, 1, dp, "b", on_x)
        send(a, 4, dp, "a", on_y)

    def own_third(a):
        send(a, 2, dp, "o", on_x)
        send(a, 5, dp, "o", on_y)

    def forward_first(a):
        got(a, 0, nbr_x, "a")
        send(a, 7, nbr_x, "a", on_y)
        send(a, 9, nbr_x, "a", on_sib)
        got(a, 3, nbr_y, "b")
        send(a, 8, nbr_y, "b", on_x)
        send(a, 12, nbr_y, "b", on_sib)

    def forward_second(a):
        got(a, 1, nbr_x, "b")
        send(a, 10, nbr_x, "b", on_sib)
        got(a, 4, nbr_y, "a")
        send(a, 13, nbr_y, "a", on_sib)

    def forward_diag(a):
        got(a, 7, diag, "a")
        send(a, 15, diag, "a", on_z)
        send(a, 17, diag, "a", on_sib)
        got(a, 8, diag, "b")
        send(a, 16, diag, "b", on_z)
        send(a, 18, diag, "b", on_sib)

    def forward_third(a):
        got(a, 2, nbr_x, "o")
        send(a, 11, nbr_x, "o", on_sib)
        got(a, 5, nbr_y, "o")
        send(a, 14, nbr_y, "o", on_sib)

    def forward_last(a):
        got(a, 15, diag, "a2")
        send(a, 19, diag, "a2", on_sib)
        got(a, 16, diag, "b2")
        send(a, 20, diag, "b2", on_sib)

    def finish_x(a):
        got(a, 9, nbr_x + to_sib, "a")
        got(a, 10, nbr_x + to_sib, "b")
        got(a, 11, nbr_x + to_sib, "o")

    def finish_y(a):
        got(a, 12, nbr_y + to_sib, "b")
        got(a, 13, nbr_y + to_sib, "a")
        got(a, 14, nbr_y + to_sib, "o")

    def finish_diag(a):
        got(a, 17, diag + to_sib, "a")
        got(a, 18, diag + to_sib, "b")
        got(a, 19, diag + to_sib, "a2")
        got(a, 20, diag + to_sib, "b2")

    def up_copy(number, owner, target):
        here = up.at[pl.ds(pl.multiple_of(owner * o_rows, 16), o_rows), :]
        return pltpu.make_async_remote_copy(
            src_ref=here, dst_ref=here, send_sem=u_send.at[number], recv_sem=u_recv.at[number],
            device_id=target, device_id_type=MESH,
        )

    def up_send(number, owner, target):
        copy = up_copy(number, owner, target)
        copy.start()
        pending.append(copy)

    own_first(0)
    up_send(0, dp, on_x)
    up_send(1, dp, on_y)
    up_send(2, dp, (diag, seq))
    up_send(3, dp, on_sib)
    own_first(1)
    own_second(0)
    send(0, 6, dp, "all", on_sib)
    send(1, 6, dp, "all", on_sib)

    place[...] = picked.astype(BF)
    place_t[...] = picked.T.astype(BF)
    for copy in local[6:]:
        copy.wait()
    for i in range(width // 128):
        gain_b[:, i * 128 : (i + 1) * 128] = gain_b_v[i : i + 1, :]
        gain_a[:, i * 128 : (i + 1) * 128] = gain_a_v[i : i + 1, :]

    def fold(v):
        return v[:, :128] + v[:, 128:]

    def spread(v):
        return jnp.broadcast_to(v, (rows, 128))

    def wide(v):
        return jnp.concatenate([v, v], axis=1)

    arrive(precv, p_send, p_recv)
    at_lane = lax.broadcasted_iota(jnp.int32, (rows, 128), 1).astype(F32)
    chosen = (precv[...].astype(F32) == at_lane).astype(F32)
    unplace[...] = chosen.astype(BF)

    @pl.loop(0, tiles, unroll=True)
    def _(n):
        csend[:, lanes(n)] = dot(unplace[...], cot[:, lanes(n)]).astype(BF)

    cot_copies = [row_copy(csend, crecv, c_send, c_recv, k) for k in range(3)]
    pending.extend(cot_copies)
    inner = (seq == 1) | (seq == 2)

    @pl.when(jnp.logical_not(inner))
    def _():
        cot_copies[1].start()
        cot_copies[2].start()

    crecv[block(seq), :] = csend[block(seq), :]
    unplace_t[...] = chosen.T.astype(BF)
    saved = [
        pltpu.make_async_copy(unplace_t, unplace_hbm, fin.at[1]),
    ]
    for copy in saved:
        copy.start()

    stat_a[...] = jnp.zeros_like(stat_a)

    @pl.loop(0, tiles, unroll=True)
    def _(n):
        v = dot(place[...], hid[:, lanes(n)])
        xs[:, lanes(n)] = v.astype(BF)
        stat_a[...] += fold(v * v)

    inv_pre = lax.rsqrt(jnp.sum(stat_a[...], axis=1, keepdims=True) / width + epsilon)
    stat_a[...] = spread(inv_pre)

    @pl.loop(0, tiles, unroll=True)
    def _(n):
        v = xs[:, lanes(n)].astype(F32) * wide(stat_a[...])
        normed[:, lanes(n)] = (v * gain_b[:, lanes(n)]).astype(BF)

    forward_first(0)
    own_third(0)
    forward_first(1)
    own_second(1)
    own_third(1)
    for k, owner in enumerate((nbr_x, nbr_y, diag)):
        up_copy(k, owner, on_sib).wait_recv()
        up_send(4 + k, owner, on_sib)
    forward_second(0)

    forward_diag(0)

    @pl.when(inner)
    def _():
        cot_copies[1].start()
        cot_copies[2].start()

    forward_third(0)
    forward_diag(1)
    cot_copies[0].start()
    forward_last(0)
    got(0, 6, sib, "all")
    finish_x(0)
    finish_y(0)
    finish_diag(0)

    low[...] = dot(normed[...], wvd[:, value_width:]).astype(BF)
    up_copy(3, sib, on_sib).wait_recv()
    for k, owner in enumerate((nbr_x, nbr_y, diag)):
        up_copy(4 + k, owner + to_sib, on_sib).wait_recv()

    @pl.loop(0, value_width // TILE, unroll=True)
    def _(n):
        proj[:, lanes(n)] = (
            dot(normed[...], wvd[:, lanes(n)]) + dot(low[...], up[lanes(n), :], 1, 1)
        ).astype(BF)

    exchange(xs, hid_e, h_send, h_recv, first=LATE, count=EARLY, stride=EARLY, order=(1, 2))
    def mix(member, init=False, last=False):
        at = pl.ds(pl.multiple_of(member // 2 * 2 * o_rows, 256), 2 * o_rows)

        @pl.loop(0, tiles, unroll=True)
        def _(n):
            m = dot(proj[:, at], wo[at, lanes(n)])
            if not init:
                m += mixed[:, lanes(n)]
            mixed[:, lanes(n)] = m
            if last:
                stat_b[...] += fold(m * m)

    stat_b[...] = jnp.zeros_like(stat_b)
    got(1, 6, sib, "all")
    mix(dp, init=True)
    forward_second(1)
    forward_last(1)
    forward_third(1)
    own_early = pl.ds(pl.multiple_of(seq * CAP + LATE, 16), EARLY)
    hid_e[block(seq, EARLY), :] = xs[own_early, :]
    hid_e[block(seq_mate, EARLY), :] = xs[own_early, :]
    exchange(proj, proj_e, q_send, q_recv, first=LATE, count=EARLY, stride=EARLY, order=(1, 2))
    proj_e[block(seq, EARLY), :] = proj[own_early, :]
    proj_e[block(seq_mate, EARLY), :] = proj[own_early, :]
    finish_diag(1)
    mix(diag)
    finish_x(1)
    mix(nbr_x)
    finish_y(1)
    mix(nbr_y, last=True)

    inv_post = lax.rsqrt(jnp.sum(stat_b[...], axis=1, keepdims=True) / width + epsilon)
    stat_b[...] = spread(inv_post)

    @pl.loop(0, tiles, unroll=True)
    def _(n):
        shaped = mixed[:, lanes(n)] * wide(stat_b[...])
        v = xs[:, lanes(n)].astype(F32) + shaped * gain_a[:, lanes(n)]
        looped[:, lanes(n)] = v.astype(BF)

    exchange(looped, loop_hbm, o_send, o_recv, count=LATE, order=(1, 2))
    exchange(looped, loop_hbm, o_send, o_recv, order=(0,))
    saved.append(
        pltpu.make_async_copy(
            looped.at[block(seq), :],
            loop_hbm.at[block(seq), :],
            fin.at[2],
        )
    )
    saved[-1].start()
    arrive(crecv, c_send, c_recv)
    stat_c[...] = jnp.zeros_like(stat_c)

    @pl.loop(0, tiles, unroll=True)
    def _(n):
        g = crecv[:, lanes(n)].astype(F32) * gain_a[:, lanes(n)]
        stat_c[...] += fold(g * (mixed[:, lanes(n)] * wide(stat_b[...])))

    pull = jnp.sum(stat_c[...], axis=1, keepdims=True) / width
    stat_c[...] = spread(pull)

    @pl.loop(0, tiles, unroll=True)
    def _(n):
        g = crecv[:, lanes(n)].astype(F32) * gain_a[:, lanes(n)]
        inv = wide(stat_b[...])
        shaped = mixed[:, lanes(n)] * inv
        gm[:, lanes(n)] = (inv * (g - shaped * wide(stat_c[...]))).astype(BF)

    @pl.loop(0, value_width // TILE, unroll=True)
    def _(n):
        gvl[:, lanes(n)] = dot(gm[...], wo[lanes(n), :], 1, 1).astype(BF)

    chip = dp // 2
    head = lsend.shape[3] - o_rows
    spans = (pl.ds(head, o_rows), pl.ds(0, head))

    def pair_copy(part):
        return pltpu.make_async_remote_copy(
            src_ref=lsend.at[:, 1 - core, :, spans[part]], dst_ref=lpair.at[:, :, spans[part]],
            send_sem=l_send.at[4 * part], recv_sem=l_recv.at[4 * part], device_id=on_sib,
            device_id_type=MESH,
        )

    def pass_on(part):
        at = spans[part]
        pair_copy(part).wait_recv()
        lsum[:, :, at] = (
            lsend[:, core, :, at].astype(F32) + lpair[:, :, at].astype(F32)
        ).astype(BF)
        for k, target in ((1, nbr_x), (2, nbr_y), (3, diag)):
            copy = pltpu.make_async_remote_copy(
                src_ref=lsum.at[target // 2, :, at], dst_ref=lrecv.at[k, :, at],
                send_sem=l_send.at[4 * part + k], recv_sem=l_recv.at[4 * part + k],
                device_id=(target, seq), device_id_type=MESH,
            )
            copy.start()
            pending.append(copy)

    cols = down_v.shape[0]

    def across(part):
        at = spans[part]
        total = lsum[chip, :, at].astype(F32)
        for k, origin in ((1, nbr_x), (2, nbr_y), (3, diag)):
            here = lrecv.at[k, :, at]
            pltpu.make_async_remote_copy(
                src_ref=here, dst_ref=here, send_sem=l_send.at[4 * part + k],
                recv_sem=l_recv.at[4 * part + k], device_id=(origin, seq), device_id_type=MESH,
            ).wait_recv()
            total += lrecv[k, :, at].astype(F32)
        zsend[:, at] = total.astype(BF)
        for k in range(1, n_seq):
            target = (seq + k) % n_seq
            copy = pltpu.make_async_remote_copy(
                src_ref=zsend.at[block(target, cols), at], dst_ref=zrecv.at[seq, :, at],
                send_sem=z_send.at[4 * part + k], recv_sem=z_recv.at[4 * part + k],
                device_id=(dp, target), device_id_type=MESH,
            )
            copy.start()
            pending.append(copy)
        zrecv[seq, :, at] = zsend[block(seq, cols), at]

    up_term = dot(low[...], gvl[:, :value_width], 0, 0).astype(BF)
    for owner in range(n_dp):
        lsend[owner // 2, owner % 2, :, head:] = up_term[:, owner * o_rows : (owner + 1) * o_rows]
    pending.append(pair_copy(0))
    pending[-1].start()
    grad_low = dot(gvl[:, :value_width], up[...]).astype(BF)
    gvl[:, value_width:] = grad_low
    down_term = dot(grad_low, normed[...], 0, 0).astype(BF)
    spare = jnp.zeros((128, head - v_rows), BF)
    for owner in range(n_dp):
        lsend[owner // 2, owner % 2, :, :head] = jnp.concatenate(
            [down_term[:, owner * v_rows : (owner + 1) * v_rows], spare], axis=1
        )
    pending.append(pair_copy(1))
    pending[-1].start()
    pass_on(0)
    pass_on(1)

    stat_c[...] = jnp.zeros_like(stat_c)

    @pl.loop(0, tiles, unroll=True)
    def _(n):
        g = dot(gvl[...], wvd[lanes(n), :], 1, 1) * gain_b[:, lanes(n)]
        mixed[:, lanes(n)] = g
        stat_c[...] += fold(g * (xs[:, lanes(n)].astype(F32) * wide(stat_a[...])))

    across(0)
    pull = jnp.sum(stat_c[...], axis=1, keepdims=True) / width
    stat_c[...] = spread(pull)

    @pl.loop(0, tiles, unroll=True)
    def _(n):
        inv = wide(stat_a[...])
        whitened = xs[:, lanes(n)].astype(F32) * inv
        g = crecv[:, lanes(n)].astype(F32) + inv * (
            mixed[:, lanes(n)] - whitened * wide(stat_c[...])
        )
        grad_v[:, lanes(n)] = dot(place_t[...], g.astype(BF)).astype(BF)

    saved.append(pltpu.make_async_copy(grad_v, grad_hbm, fin.at[3]))
    saved[-1].start()

    across(1)

    arrive(hid_e, h_send, h_recv, count=EARLY, stride=EARLY, order=(1, 2))
    arrive(proj_e, q_send, q_recv, count=EARLY, stride=EARLY, order=(1, 2))
    stat_e[...] = jnp.zeros_like(stat_e)

    @pl.loop(0, tiles, unroll=True)
    def _(n):
        m = dot(proj_e[...], wo[:, lanes(n)])
        mixed_e[:, lanes(n)] = m
        stat_e[...] += fold(m * m)

    inv_early = lax.rsqrt(jnp.sum(stat_e[...], axis=1, keepdims=True) / width + epsilon)
    stat_e[...] = jnp.broadcast_to(inv_early, stat_e.shape)

    @pl.loop(0, tiles, unroll=True)
    def _(n):
        shaped = mixed_e[:, lanes(n)] * wide(stat_e[...])
        v = hid_e[:, lanes(n)].astype(F32) + shaped * gain_a[:, lanes(n)]
        looped_e[:, lanes(n)] = v.astype(BF)

    for i in (1, 2):
        saved.append(
            pltpu.make_async_copy(
                looped_e.at[block(peers[i], EARLY), :],
                loop_hbm.at[pl.ds(pl.multiple_of(peers[i] * CAP + LATE, 16), EARLY), :],
                fin.at[4 + i],
            )
        )
        saved[-1].start()

    for part, at in enumerate(spans):
        for k in range(1, n_seq):
            origin = (seq + n_seq - k) % n_seq
            here = zrecv.at[origin, :, at]
            pltpu.make_async_remote_copy(
                src_ref=here, dst_ref=here, send_sem=z_send.at[4 * part + k],
                recv_sem=z_recv.at[4 * part + k], device_id=(dp, origin), device_id_type=MESH,
            ).wait_recv()
    grad_scale = 1.0 / math.sqrt(n_seq * cot.shape[0] * n_dp)
    part = [zrecv[i].astype(F32) for i in range(n_seq)]
    mine = ((part[0] + part[1]) + (part[2] + part[3])) * grad_scale
    down_v[...] = mine[:, :v_rows]
    up_v[...] = mine[:, lsend.shape[3] - o_rows :]
    saved.append(pltpu.make_async_copy(down_v, down_hbm, fin.at[8]))
    saved.append(pltpu.make_async_copy(up_v, up_hbm, fin.at[9]))
    saved[-2].start()
    saved[-1].start()

    arrive(loop_hbm, o_send, o_recv, count=LATE, order=(1, 2))
    arrive(loop_hbm, o_send, o_recv, order=(0,))
    for copy in pending:
        copy.wait_send()
    for copy in saved:
        copy.wait()


def store_kernel(
    grad_in, loop_in, unplace_in, down_in, up_in, looped_hbm, grad_hbm, down_hbm, up_hbm,
    grad_v, loop_v, unplace_v, down_v, up_v, looped_o, ins, outs,
):
    moves = [
        (unplace_in, unplace_v, None),
        (loop_in, loop_v, None),
        (grad_in, grad_v, grad_hbm),
        (down_in, down_v, down_hbm),
        (up_in, up_v, up_hbm),
    ]
    loads = [pltpu.make_async_copy(a, b, ins.at[i]) for i, (a, b, _) in enumerate(moves)]
    for copy in loads:
        copy.start()
    stores = [pltpu.make_async_copy(moves[i][1], moves[i][2], outs.at[i]) for i in (2, 3, 4)]
    loads[0].wait()
    loads[1].wait()
    width = loop_v.shape[1]
    half = width // 2
    for k in range(2):
        at = pl.ds(k * half, half)
        looped_o[:, at] = dot(unplace_v[...], loop_v[:, at]).astype(BF)
        stores.append(
            pltpu.make_async_copy(looped_o.at[:, at], looped_hbm.at[:, at], outs.at[k])
        )
        stores[-1].start()
        if k == 0:
            for i in (2, 3, 4):
                loads[i].wait()
                stores[i - 2].start()
    for copy in stores:
        copy.wait()


def fused_body(
    hidden, depths, packed_slot_index, value_weight, output_weight, adapter_down_factor,
    adapter_up_factor, before_norm_gain, after_norm_gain, cotangent,
):
    tok, width = hidden.shape
    act = cotangent.shape[0]
    n_dp, n_seq = lax.axis_size("dp"), lax.axis_size("seq")
    v_rows, value_width = value_weight.shape
    o_rows = output_weight.shape[0]
    rank = adapter_up_factor.shape[1]
    cols = rank // n_seq
    lead = -(-v_rows // 128) * 128 + o_rows
    vm, hbm = pl.BlockSpec(memory_space=pltpu.VMEM), pl.BlockSpec(memory_space=pltpu.HBM)
    dma = pltpu.SemaphoreType.DMA
    rows = n_seq * CAP

    def b16(*shape):
        return pltpu.VMEM(shape, BF)

    def f32(*shape):
        return pltpu.VMEM(shape, F32)

    sh = jax.ShapeDtypeStruct
    lora = (sh((cols, v_rows), F32), sh((cols, o_rows), F32))
    between = (
        sh((tok, width), BF), sh((rows, width), BF), sh((act, rows), BF),
    ) + lora
    early = n_seq * EARLY
    results = pl.pallas_call(
        fused_kernel,
        out_shape=between,
        in_specs=[hbm] * 10,
        out_specs=(hbm,) * 5,
        scratch_shapes=[
            pltpu.VMEM((tok // 128, 128), jnp.int32),
            pltpu.VMEM((tok // 128, 128), jnp.int32),
            f32(width // 128, 128),
            f32(width // 128, 128),
            b16(tok, width),
            b16(act, width),
            b16(v_rows * n_dp, value_width + rank),
            b16(o_rows * n_dp, width),
            b16(o_rows * n_dp, rank),
            b16(rows, 128),
            b16(rows, 128),
            b16(rows, width),
            b16(rows, width),
            f32(1, width),
            f32(1, width),
            b16(rows, width),
            b16(rows, width),
            b16(rows, value_width),
            b16(rows, rank),
            f32(rows, width),
            b16(rows, width),
            b16(rows, value_width + rank),
            b16(rows, width),
            b16(tok, rows),
            b16(rows, tok),
            b16(rows, 128),
            b16(128, rows),
            b16(n_dp // 2, 2, rank, lead),
            b16(n_dp // 2, rank, lead),
            b16(n_dp // 2, rank, lead),
            b16(4, rank, lead),
            b16(rank, lead),
            b16(n_seq, cols, lead),
            f32(rows, 128),
            f32(rows, 128),
            f32(rows, 128),
            f32(early, 128),
            b16(early, width),
            b16(early, value_width),
            f32(early, width),
            b16(early, width),
            b16(rows, width),
            f32(cols, v_rows),
            f32(cols, o_rows),
        ]
        + [dma((n,)) for n in (42, 42, 8, 8) + (4,) * 10 + (8, 8, 8, 8, 10, 10)],
        compiler_params=pltpu.CompilerParams(
            collective_id=0, has_side_effects=True, vmem_limit_bytes=56 << 20
        ),
        name="layer",
    )(
        packed_slot_index.reshape(tok // 128, 128),
        depths.reshape(tok // 128, 128),
        before_norm_gain.reshape(width // 128, 128),
        after_norm_gain.reshape(width // 128, 128),
        hidden,
        cotangent,
        value_weight,
        output_weight,
        adapter_down_factor,
        adapter_up_factor,
    )
    looped, grad, down, up = pl.pallas_call(
        store_kernel,
        out_shape=(sh((act, width), BF), sh((tok, width), BF)) + lora,
        in_specs=[hbm] * 5,
        out_specs=(hbm,) * 4,
        scratch_shapes=[
            b16(tok, width),
            b16(rows, width),
            b16(act, rows),
            f32(cols, v_rows),
            f32(cols, o_rows),
            b16(act, width),
            dma((5,)),
            dma((5,)),
        ],
        compiler_params=pltpu.CompilerParams(vmem_limit_bytes=56 << 20),
        name="store",
    )(*results)
    return looped, grad, down.T, up.T


def body(*arrays):
    fits = (
        lax.axis_size("dp") == 8
        and lax.axis_size("seq") == 4
        and arrays[0].shape[0] == 4 * CAP
        and arrays[9].shape[0] == 128
        and arrays[0].shape[1] % 256 == 0
        and arrays[3].shape[1] % 256 == 0
        and all(arrays[i].shape[0] % 32 == 0 for i in (3, 4, 5, 6))
        and arrays[4].shape[0] == 128
        and arrays[6].shape[1] == 128
    )
    return (fused_body if fits else general_body)(*arrays)


def solution(mesh):
    placed = (
        P(("dp", "seq"), None),
        P(("dp", "seq")),
        P(("dp", "seq")),
        P("dp", None),
        P("dp", None),
        P("dp", None),
        P("dp", None),
        P(),
        P(),
        P(("dp", "seq"), None),
    )
    return jax.shard_map(
        body,
        mesh=mesh,
        in_specs=placed,
        out_specs=(P(("dp", "seq"), None), P(("dp", "seq"), None), P("dp", "seq"), P("dp", "seq")),
        check_vma=False,
    )
```
